256 devices in a mesh: ka: 64 (over z, y_lo, x), ga: 4 (over y_hi, core).
Axes of the slice: x: 4, y: 4 (y_hi: 2, y_lo: 2; y = y_hi * 2 + y_lo), z: 8, core: 2. Of those that a mesh axis runs over, the one named last changes fastest.
Arguments:
- orbitals: bfloat16 [2, 256, 128, 4096], P(None, 'ka', None, 'ga')
- gauge: bfloat16 [2, 256, 128, 128], P(None, 'ka'), may hold values from -0.5 to 0.5
- neighbour: int32 [256, 3], replicated, may hold values from 0 to 255, as said below
- wrap_shift: int32 [256, 3, 3], replicated, may hold values from 0 to 1, as said below
Outputs:
- forward: float32 [3, 2, 256, 128, 128], P(None, None, 'ka')
- backward: float32 [3, 2, 256, 128, 128], P(None, None, 'ka')
The draws below stay inside these ranges and needn't reach their ends.
Inputs may be any that keep to these rules, and one draw needn't show every extreme that they name: The k point k lies on device k // 4 of ka, whose index is d = j * 4 + i. For each direction b the map k -> neighbour[k, b] is a permutation; neighbour[k, 0] lies on the same device, neighbour[k, 1] on device j * 4 + (i + 1) % 4, neighbour[k, 2] on device (d + 4) % 64. wrap_shift[k, b, d] is zero for d != b.
All inputs are finite; a program needn't handle non-finite values.
Results may differ from the reference program's by a relative error of at most 0.00084.
Values may be sent and summed in bfloat16 or wider, within the bound.
No kernel may reach another device: no remote copies, remote signals or barrier semaphores. Data moves between devices by JAX's collectives and lax.ppermute only.
A program may use at most 64 MiB of HBM per device.

```python
import math
import jax
import jax.numpy as jnp
from jax import lax

NB = 128
KLOC = 4
KRING = 4
GY = 32
GZ = 32
NK = 256
NGRID = 4096


def neighbour_layout(key):
    device_count = NK // KLOC
    scores = jax.random.randint(jax.random.fold_in(key, 7), (device_count, KLOC), 0, 1 << 20) * KLOC + jnp.arange(KLOC, dtype=jnp.int32)[None, :]
    coord = jnp.argsort(scores, axis=1).astype(jnp.int32)
    slot_of = jnp.argsort(coord, axis=1).astype(jnp.int32)
    device = jnp.arange(device_count, dtype=jnp.int32)[:, None] + jnp.zeros((1, KLOC), jnp.int32)
    cycle = device % KRING
    outer = device // KRING
    outer_count = device_count // KRING
    first_dev = device
    first_coord = (coord + 1) % KLOC
    second_dev = outer * KRING + (cycle + 1) % KRING
    third_dev = (device + KRING) % device_count
    first_next = first_dev * KLOC + slot_of[first_dev, first_coord]
    second_next = second_dev * KLOC + slot_of[second_dev, coord]
    third_next = third_dev * KLOC + slot_of[third_dev, coord]
    table = jnp.stack([first_next, second_next, third_next], axis=-1).reshape(NK, 3).astype(jnp.int32)
    wraps = jnp.stack([coord == KLOC - 1, cycle == KRING - 1, outer == outer_count - 1], axis=-1).reshape(NK, 3).astype(jnp.int32)
    shifts = wraps[:, :, None] * jnp.eye(3, dtype=jnp.int32)[None, :, :]
    return (table, shifts)


def draw_neighbour(key, part):
    return neighbour_layout(key)[0]


def draw_wrap_shift(key, part):
    return neighbour_layout(key)[1]


def draw_orbitals(key, part):
    common_key, own_key = jax.random.split(jax.random.fold_in(key, 11))
    common = jax.random.normal(common_key, (2, 1, NB, NGRID), jnp.float32)
    own = jax.random.normal(own_key, (2, NK, NB, NGRID), jnp.float32)
    mixed = 0.8 * common + 0.6 * own
    return (mixed / jnp.sqrt(jnp.float32(NGRID))).astype(jnp.bfloat16)


def block_scale(key, shape, cuts, low, largest):
    def one(position, blocks):
        steps = jax.random.uniform(jax.random.fold_in(jax.random.fold_in(key, 6), position), (blocks,), jnp.float32, low / len(cuts), largest / len(cuts))
        return jnp.repeat(jnp.exp(steps), shape[position] // blocks).reshape((-1,) + (1,) * (len(shape) - position - 1))

    factor_of = one(*cuts[0])
    for cut in cuts[1:]:
        factor_of = factor_of * one(*cut)
    return factor_of


def scatter_about(stream_key, dims, scale, reach, cuts=(), kind=jnp.bfloat16):
    level = block_scale(stream_key, dims, cuts, -0.22, 0.18) if cuts else 1.0
    values = jax.random.normal(stream_key, dims, jnp.float32) * scale * level
    return jnp.minimum(jnp.maximum(values, -reach), reach).astype(kind)


def setup_inputs(seed: int = 0) -> dict:
    streams_of = jax.random.split(jax.random.key(seed), 5)
    return {
        "orbitals": draw_orbitals(jax.random.fold_in(streams_of[4], 71), 0),
        "gauge": scatter_about(streams_of[1], (2, NK, NB, NB), NB ** -0.5, 0.5, ((1, 64),)),
        "neighbour": draw_neighbour(jax.random.fold_in(streams_of[4], 71), 0),
        "wrap_shift": draw_wrap_shift(jax.random.fold_in(streams_of[4], 71), 0),
    }


def grid_fractions(plane_first, plane_count, plane_total):
    point_index = jnp.arange(plane_count * GY * GZ, dtype=jnp.int32)
    plane = point_index // (GY * GZ) + plane_first
    middle = (point_index // GZ) % GY
    inner = point_index % GZ
    return [plane.astype(jnp.float32) / jnp.float32(plane_total), middle.astype(jnp.float32) / jnp.float32(GY), inner.astype(jnp.float32) / jnp.float32(GZ)]


def phase_angles(shift_rows, direction, mesh_counts, fractions):
    total = jnp.zeros((shift_rows.shape[0], fractions[0].shape[0]), jnp.float32)
    for lattice in range(3):
        step = 1.0 / mesh_counts[lattice] if lattice == direction else 0.0
        wave = shift_rows[:, lattice].astype(jnp.float32) + jnp.float32(step)
        total = total + wave[:, None] * fractions[lattice][None, :]
    return jnp.float32(2.0 * math.pi) * total


def phase_apply(angles, source):
    cosine = jnp.cos(angles)[:, None, :]
    sine = jnp.sin(angles)[:, None, :]
    source_re = source[0].astype(jnp.float32)
    source_im = source[1].astype(jnp.float32)
    return jnp.stack([cosine * source_re + sine * source_im, cosine * source_im - sine * source_re]).astype(jnp.bfloat16)


def split_parts(values):
    high = values.astype(jnp.bfloat16)
    back = lax.optimization_barrier(high).astype(jnp.float32)
    low = (values - back).astype(jnp.bfloat16)
    return high, low


def rotate_blocks(blocks, left, right):
    highest = lax.Precision.HIGHEST

    def times(first, second):
        high, low = split_parts(first)
        wide = second.astype(jnp.float32)
        return jnp.einsum('kab,kbc->kac', high.astype(jnp.float32), wide, precision=highest) + jnp.einsum('kab,kbc->kac', low.astype(jnp.float32), wide, precision=highest)

    def adjoint(first, second):
        high, low = split_parts(second)
        wide = first.astype(jnp.float32)
        return jnp.einsum('kba,kbc->kac', wide, high.astype(jnp.float32), precision=highest) + jnp.einsum('kba,kbc->kac', wide, low.astype(jnp.float32), precision=highest)

    temp_re = times(blocks[0], right[0]) - times(blocks[1], right[1])
    temp_im = times(blocks[0], right[1]) + times(blocks[1], right[0])
    out_re = adjoint(left[0], temp_re) + adjoint(left[1], temp_im)
    out_im = adjoint(left[0], temp_im) - adjoint(left[1], temp_re)
    return jnp.stack([out_re, out_im])


def reference(orbitals, gauge, neighbour, wrap_shift):
    total_k = orbitals.shape[1]
    plane_total = NGRID // (GY * GZ)
    fractions = grid_fractions(0, plane_total, plane_total)
    counts = (KLOC, KRING, total_k // (KLOC * KRING))

    def one_point(kpoint):
        own = lax.dynamic_index_in_dim(orbitals, kpoint, 1, keepdims=False)
        blocks = []
        for direction in range(3):
            target = neighbour[kpoint, direction]
            shift_row = lax.dynamic_index_in_dim(wrap_shift[:, direction, :], kpoint, 0, keepdims=True)
            angles = phase_angles(shift_row, direction, counts, fractions)
            source = lax.dynamic_index_in_dim(orbitals, target, 1, keepdims=True)
            phased = phase_apply(angles, source)
            phased_re = phased[0, 0]
            phased_im = phased[1, 0]
            block_re = jnp.dot(own[0], phased_re.T, preferred_element_type=jnp.float32) + jnp.dot(own[1], phased_im.T, preferred_element_type=jnp.float32)
            block_im = jnp.dot(own[0], phased_im.T, preferred_element_type=jnp.float32) - jnp.dot(own[1], phased_re.T, preferred_element_type=jnp.float32)
            blocks.append(jnp.stack([block_re, block_im]))
        return jnp.stack(blocks)

    raw = lax.map(one_point, jnp.arange(total_k, dtype=jnp.int32))
    raw = jnp.transpose(raw, (1, 2, 0, 3, 4))
    rotated = []
    returned = []
    for direction in range(3):
        right = jnp.take(gauge, neighbour[:, direction], axis=1)
        block = rotate_blocks(raw[direction], gauge, right)
        rotated.append(block)
        inverse = jnp.zeros((total_k,), jnp.int32).at[neighbour[:, direction]].set(jnp.arange(total_k, dtype=jnp.int32))
        partner = jnp.take(block, inverse, axis=1)
        returned.append(jnp.stack([jnp.swapaxes(partner[0], -1, -2), -jnp.swapaxes(partner[1], -1, -2)]))
    return jnp.stack(rotated), jnp.stack(returned)
```

```python
import math

import jax
import jax.numpy as jnp
from jax import lax
from jax.experimental import pallas as pl
from jax.experimental.pallas import tpu as pltpu
from jax.sharding import PartitionSpec as P

KRING = 4
GY = 32
GZ = 32
F32 = jnp.float32
BF16 = jnp.bfloat16
CONTRACT_LAST = (((1,), (1,)), ((), ()))
CONTRACT_FIRST = (((0,), (0,)), ((), ()))


def grid_fractions(plane_first, plane_count, plane_total):
    point_index = jnp.arange(plane_count * GY * GZ, dtype=jnp.int32)
    plane = point_index // (GY * GZ) + plane_first
    middle = point_index // GZ % GY
    inner = point_index % GZ
    return [
        plane.astype(F32) / F32(plane_total),
        middle.astype(F32) / F32(GY),
        inner.astype(F32) / F32(GZ),
    ]


def phase_angles(shift_rows, direction, mesh_counts, fractions):
    total = jnp.zeros((shift_rows.shape[0], fractions[0].shape[0]), F32)
    for lattice in range(3):
        step = 1.0 / mesh_counts[lattice] if lattice == direction else 0.0
        wave = shift_rows[:, lattice].astype(F32) + F32(step)
        total = total + wave[:, None] * fractions[lattice][None, :]
    return F32(2.0 * math.pi) * total


def correlate_pair(own, source, twiddle, slot, k, phased):
    nb = own.shape[2]
    cosine = twiddle[0:1, :]
    sine = twiddle[1:2, :]
    source_re = source[0, slot].astype(F32)
    source_im = source[1, slot].astype(F32)
    phased[0:nb, :] = (cosine * source_re + sine * source_im).astype(BF16)
    phased[nb:, :] = (cosine * source_im - sine * source_re).astype(BF16)
    left = jnp.concatenate([own[0, k], own[1, k]], axis=0)
    full = lax.dot_general(left, phased[...], CONTRACT_LAST, preferred_element_type=F32)
    return full[:nb, :nb] + full[nb:, nb:], full[:nb, nb:] - full[nb:, :nb]


def correlate_own_body(meta, twiddle, orbitals, give, keep, own, phased, sem):
    copy = pltpu.make_async_copy(orbitals, own, sem)
    copy.start()
    copy.wait()
    for p in range(4):
        k = meta[1, p]
        out = give if p < 2 else keep
        out[p % 2, 0], out[p % 2, 1] = correlate_pair(own, own, twiddle.at[k], meta[0, p], k, phased.at[p % 2])


def correlate_own(meta, twiddle, orbitals):
    nb, points = orbitals.shape[2:]
    half = jax.ShapeDtypeStruct((2, 2, nb, nb), F32)
    vmem = pl.BlockSpec(memory_space=pltpu.VMEM)
    return pl.pallas_call(
        correlate_own_body,
        out_shape=(half, half, pltpu.VMEM(orbitals.shape, BF16)),
        in_specs=[pl.BlockSpec(memory_space=pltpu.SMEM), vmem, pl.BlockSpec(memory_space=pl.ANY)],
        out_specs=(vmem, vmem, vmem),
        scratch_shapes=[pltpu.VMEM((2, 2 * nb, points), BF16), pltpu.SemaphoreType.DMA],
        cost_estimate=pl.CostEstimate(flops=4 * 8 * nb * nb * points, bytes_accessed=2**22, transcendentals=0),
    )(meta, twiddle, orbitals)


def correlate_body(meta, twiddle_x, twiddle_y, own, beside, beyond, give, keep, source, phased, sems):
    copies = [pltpu.make_async_copy(a, source.at[n], sems.at[n]) for n, a in enumerate((beside, beyond))]
    for copy in copies:
        copy.start()
    for n, twiddle in enumerate((twiddle_x, twiddle_y)):
        copies[n].wait()
        for p in (n, 2 + n):
            k = meta[1, p]
            out = give if p < 2 else keep
            out[n, 0], out[n, 1] = correlate_pair(own, source.at[n], twiddle.at[k], meta[0, p], k, phased.at[p // 2])


def correlate(meta, twiddle_x, twiddle_y, own, beside, beyond):
    nb, points = own.shape[2:]
    half = jax.ShapeDtypeStruct((2, 2, nb, nb), F32)
    vmem = pl.BlockSpec(memory_space=pltpu.VMEM)
    hbm = pl.BlockSpec(memory_space=pl.ANY)
    return pl.pallas_call(
        correlate_body,
        out_shape=(half, half),
        in_specs=[pl.BlockSpec(memory_space=pltpu.SMEM), vmem, vmem, vmem, hbm, hbm],
        out_specs=(vmem, vmem),
        scratch_shapes=[
            pltpu.VMEM((2, *beside.shape), BF16),
            pltpu.VMEM((2, 2 * nb, points), BF16),
            pltpu.SemaphoreType.DMA((2,)),
        ],
        cost_estimate=pl.CostEstimate(flops=4 * 8 * nb * nb * points, bytes_accessed=2**22, transcendentals=0),
    )(meta, twiddle_x, twiddle_y, own, beside, beyond)


def split_parts(values):
    high = values.astype(BF16)
    low = (values - high.astype(F32)).astype(BF16)
    return high, low


def rotate_pair(raw_parts, left, right):
    nb = left[0].shape[0]
    raw_re, raw_im = [jnp.concatenate(split_parts(part), axis=1) for part in raw_parts]
    raw = jnp.concatenate([raw_re, raw_im], axis=0)
    wide = jnp.concatenate(right, axis=1)
    prod = jnp.dot(raw, jnp.concatenate([wide, wide], axis=0), preferred_element_type=F32)
    temp_re = prod[:nb, :nb] - prod[nb:, nb:]
    temp_im = prod[:nb, nb:] + prod[nb:, :nb]
    re_high, re_low = split_parts(temp_re)
    im_high, im_low = split_parts(temp_im)
    temp = jnp.concatenate(
        [jnp.concatenate([re_high, im_high], axis=1), jnp.concatenate([re_low, im_low], axis=1)], axis=0
    )
    tall = jnp.concatenate(left, axis=1)
    prod = lax.dot_general(
        jnp.concatenate([tall, tall], axis=0), temp, CONTRACT_FIRST, preferred_element_type=F32
    )
    return prod[:nb, :nb] + prod[nb:, nb:], prod[:nb, nb:] - prod[nb:, :nb]


def rotate(meta, mine, other, left, rights, right_of, layout):
    nb = left.shape[2]
    pairs = len(right_of)
    vmem = pl.BlockSpec(memory_space=pltpu.VMEM)

    def body(slots, mine, other, left, *refs):
        rights_in, outs = refs[: len(rights)], refs[len(rights) :]
        for p in range(pairs):
            k = slots[1, p]
            n = slots[2, p]
            right = rights_in[right_of[p]]
            out_re, out_im = rotate_pair(
                [mine[p, c] + other[p, c] for c in range(2)],
                [left[c, k] for c in range(2)],
                [right[c, n] for c in range(2)],
            )
            for out, rows in zip(outs, layout):
                for row, (pair, adjoint) in enumerate(rows):
                    if pair == p and adjoint:
                        out[row, 0] = out_re.T
                        out[row, 1] = -out_im.T
                    elif pair == p:
                        out[row, 0] = out_re
                        out[row, 1] = out_im

    return pl.pallas_call(
        body,
        out_shape=tuple(jax.ShapeDtypeStruct((len(rows), 2, nb, nb), F32) for rows in layout),
        in_specs=[pl.BlockSpec(memory_space=pltpu.SMEM)] + [vmem] * (3 + len(rights)),
        out_specs=(vmem,) * len(layout),
        cost_estimate=pl.CostEstimate(flops=pairs * 4 * 256**3, bytes_accessed=pairs * 2**19, transcendentals=0),
    )(meta, mine, other, left, *rights)


def place(targets, meta, blocks, outs):
    nb = blocks[0].shape[-1]
    shape = jax.ShapeDtypeStruct((3, 2, 4, nb, nb), F32)
    previous = () if outs is None else tuple(outs)
    vmem = pl.BlockSpec(memory_space=pltpu.VMEM)
    hbm = pl.BlockSpec(memory_space=pl.ANY)

    def body(slots, *refs):
        sems = refs[-1]
        into = refs[-3:-1]
        copies = []
        for block, rows in zip(refs, targets):
            for n, (output, direction, slot) in enumerate(rows):
                target = into[output].at[direction, :, slots[slot]]
                copies.append(pltpu.make_async_copy(block.at[n], target, sems.at[len(copies)]))
        for copy in copies:
            copy.start()
        for copy in copies:
            copy.wait()

    count = len(blocks)
    total = sum(len(rows) for rows in targets)
    return pl.pallas_call(
        body,
        out_shape=(shape, shape),
        in_specs=[pl.BlockSpec(memory_space=pltpu.SMEM)] + [vmem] * count + [hbm] * len(previous),
        out_specs=(hbm, hbm),
        scratch_shapes=[pltpu.SemaphoreType.DMA((total,))],
        input_output_aliases={1 + count: 0, 2 + count: 1} if previous else {},
        cost_estimate=pl.CostEstimate(flops=0, bytes_accessed=total * 2**18, transcendentals=0),
    )(meta, *blocks, *previous)


def shards(orbitals, gauge, neighbour, wrap_shift):
    kloc = orbitals.shape[1]
    nb = orbitals.shape[2]
    grid_points = orbitals.shape[3]
    ka_count = lax.axis_size("ka")
    ga_count = lax.axis_size("ga")
    device = lax.axis_index("ka")
    grid_part = lax.axis_index("ga")
    core = grid_part % 2
    plane_count = grid_points // (GY * GZ)
    counts = (kloc, KRING, ka_count // KRING)

    ring_back = [(d, d // KRING * KRING + (d - 1) % KRING) for d in range(ka_count)]
    outer_back = [(d, (d - KRING) % ka_count) for d in range(ka_count)]
    ring_ahead = [(t, s) for s, t in ring_back]
    outer_ahead = [(t, s) for s, t in outer_back]
    sibling = [(g, g ^ 1) for g in range(ga_count)]
    ring_ahead_sibling = [
        (s * ga_count + g, t * ga_count + (g ^ 1)) for s, t in ring_ahead for g in range(ga_count)
    ]
    across = [(g, g ^ 2) for g in range(ga_count)]

    gauge_half = lax.dynamic_index_in_dim(gauge.reshape(2, 2, 2, nb, nb), core, 2, keepdims=False)
    gauge_beside = lax.ppermute(gauge_half, "ka", ring_back)
    gauge_beyond = lax.ppermute(gauge_half, "ka", outer_back)
    front = orbitals[:, :2]
    rear = orbitals[:, 2:]
    beyond_front = lax.ppermute(front, "ka", outer_back)
    beside_front = lax.ppermute(front, "ka", ring_back)
    beyond_rear = lax.ppermute(rear, "ka", outer_back)
    beside_rear = lax.ppermute(rear, "ka", ring_back)

    fractions = grid_fractions(grid_part * plane_count, plane_count, plane_count * ga_count)
    my_table = lax.dynamic_slice_in_dim(neighbour, device * kloc, kloc, 0) % kloc
    my_shift = lax.dynamic_slice_in_dim(wrap_shift, device * kloc, kloc, 0)
    slots = jnp.arange(kloc, dtype=jnp.int32)
    local = jnp.stack([1 - core, 1 - core, core, core]).astype(jnp.int32)

    def k_slots(direction, wanted):
        match = my_table[:, direction][:, None] == wanted[None, :]
        return jnp.sum(jnp.where(match, slots[:, None], 0), axis=0)

    pair_is_first = slots % 2 == 0
    order = local + jnp.where(pair_is_first, 0, 2)
    meta_own = jnp.stack([order, k_slots(0, order), order, order])

    def meta_of(part):
        wanted = local + 2 * part
        k = jnp.where(pair_is_first, k_slots(1, wanted), k_slots(2, wanted))
        return jnp.stack([local, k, jnp.full((kloc,), part, jnp.int32), wanted])

    angles = [phase_angles(my_shift[:, b, :], b, counts, fractions) for b in range(3)]
    twiddles = [jnp.stack([jnp.cos(a), jnp.sin(a)], axis=1) for a in angles]

    def gather_sum(give, keep):
        return keep + lax.ppermute(give, "ga", sibling)

    give, keep, own = correlate_own(meta_own, twiddles[0], orbitals)
    got = lax.ppermute(give, "ga", sibling)
    meta_front, meta_rear = meta_of(0), meta_of(1)
    give_front, keep_front = correlate(meta_front, twiddles[1], twiddles[2], own, beside_front, beyond_front)
    got_front = lax.ppermute(give_front, "ga", sibling)
    chip = jnp.concatenate([keep + got, keep_front + got_front], axis=0)
    other = lax.ppermute(chip, "ga", across)

    chip, beside_rear, beyond_rear = lax.optimization_barrier((chip, beside_rear, beyond_rear))
    give, keep = correlate(meta_rear, twiddles[1], twiddles[2], own, beside_rear, beyond_rear)
    chip_rear = keep + lax.ppermute(give, "ga", sibling)
    other_rear = lax.ppermute(chip_rear, "ga", across)

    other, chip_rear = lax.optimization_barrier((other, chip_rear))
    meta_first = jnp.concatenate([meta_own[:, 2:], meta_front[:, 2:]], axis=1)
    first, adj_x, adj_y = rotate(
        meta_first, chip, other, gauge, (gauge, gauge_beside, gauge_beyond), (0, 0, 1, 2),
        [[(0, 0), (1, 0), (2, 0), (3, 0), (0, 1), (1, 1)], [(2, 1)], [(3, 1)]],
    )

    def deliver(fwd, adj_x, adj_y):
        adj_y = lax.ppermute(adj_y, "ka", outer_ahead)
        adj_x, adj_x_sib = lax.ppermute(adj_x, "ka", ring_ahead), lax.ppermute(adj_x, ("ka", "ga"), ring_ahead_sibling)
        fwd_sib = lax.ppermute(fwd, "ga", sibling)
        return fwd, fwd_sib, adj_x, adj_x_sib, adj_y, lax.ppermute(adj_y, "ga", sibling)

    blocks = deliver(first, adj_x, adj_y)
    meta_second = meta_rear[:, 2:]
    last, adj_x, adj_y = rotate(
        meta_second, chip_rear, other_rear, gauge, (gauge_beside, gauge_beyond), (0, 1),
        [[(0, 0), (1, 0)], [(0, 1)], [(1, 1)]],
    )
    last, *blocks = lax.optimization_barrier((last, *blocks))
    blocks_rear = deliver(last, adj_x, adj_y)

    k_own, k_front, k_rear = meta_own[1], meta_front[1], meta_rear[1]
    s_own, s_front, s_rear = meta_own[3], meta_front[3], meta_rear[3]
    where = jnp.concatenate([k_own, s_own, k_front, s_front])
    targets = []
    for base in (2, 0):
        targets.append(
            [(0, 0, base), (0, 0, base + 1), (0, 1, base + 8), (0, 2, base + 9), (1, 0, base + 4), (1, 0, base + 5)]
        )
    targets += [[(1, 1, 14)], [(1, 1, 12)], [(1, 2, 15)], [(1, 2, 13)]]
    outs = place(targets, where, blocks, None)
    where = jnp.concatenate([k_rear, s_rear])
    targets = [[(0, 1, 2), (0, 2, 3)], [(0, 1, 0), (0, 2, 1)], [(1, 1, 6)], [(1, 1, 4)], [(1, 2, 7)], [(1, 2, 5)]]
    return tuple(place(targets, where, blocks_rear, outs))


def solution(mesh):
    in_specs = (P(None, "ka", None, "ga"), P(None, "ka", None, None), P(), P())
    out_specs = (P(None, None, "ka", None, None), P(None, None, "ka", None, None))
    return jax.shard_map(shards, mesh=mesh, in_specs=in_specs, out_specs=out_specs, check_vma=False)
```

```python
import math

import jax
import jax.numpy as jnp
from jax import lax
from jax.experimental import pallas as pl
from jax.experimental.pallas import tpu as pltpu
from jax.sharding import PartitionSpec as P

KRING = 4
GY = 32
GZ = 32
F32 = jnp.float32
BF16 = jnp.bfloat16
PACKED_ROWS = 16
SHIFT = 13
VMEM = pltpu.VMEM
CONTRACT_LAST = (((1,), (1,)), ((), ()))
CONTRACT_FIRST = (((0,), (0,)), ((), ()))


def grid_fractions(plane_first, plane_count, plane_total):
    point_index = jnp.arange(plane_count * GY * GZ, dtype=jnp.int32)
    plane = point_index // (GY * GZ) + plane_first
    middle = point_index // GZ % GY
    inner = point_index % GZ
    return [
        plane.astype(F32) / F32(plane_total),
        middle.astype(F32) / F32(GY),
        inner.astype(F32) / F32(GZ),
    ]


def phase_angles(shift_rows, direction, mesh_counts, fractions):
    total = jnp.zeros((shift_rows.shape[0], fractions[0].shape[0]), F32)
    for lattice in range(3):
        step = 1.0 / mesh_counts[lattice] if lattice == direction else 0.0
        wave = shift_rows[:, lattice].astype(F32) + F32(step)
        total = total + wave[:, None] * fractions[lattice][None, :]
    return F32(2.0 * math.pi) * total


def vmem(*arrays):
    return tuple(pltpu.with_memory_space_constraint(array, VMEM) for array in arrays)


def specs(*spaces):
    return [pl.BlockSpec(memory_space=space) for space in spaces]


def small(mib):
    return {
        "cost_estimate": pl.CostEstimate(flops=1, bytes_accessed=1, transcendentals=0),
        "compiler_params": pltpu.CompilerParams(vmem_limit_bytes=mib * 2**20),
    }


def load(core, orbitals, gauge, part):
    nb, points = orbitals.shape[2:]
    blocks = points // nb

    def body(core, orbitals, gauge, out, block, sems):
        copies = [
            pltpu.make_async_copy(
                orbitals.at[c, 2 * part + slot], out.at[c, slot * nb : (slot + 1) * nb], sems.at[2 * c + slot]
            )
            for c in range(2)
            for slot in range(2)
        ]
        copies.append(pltpu.make_async_copy(gauge.at[:, 2 * part + core[0]], block, sems.at[4]))
        for copy in copies:
            copy.start()
        copies[4].wait()
        for c in range(2):
            for j in range(blocks):
                rows = block[c, j * PACKED_ROWS : (j + 1) * PACKED_ROWS, :]
                out[c, 2 * nb :, j * nb : (j + 1) * nb] = rows
        for copy in copies[:4]:
            copy.wait()

    return pl.pallas_call(
        body,
        name="load",
        out_shape=VMEM((2, 2 * nb + PACKED_ROWS, points), BF16),
        in_specs=specs(pltpu.SMEM, pl.ANY, pl.ANY),
        out_specs=specs(VMEM)[0],
        scratch_shapes=[VMEM((2, nb, nb), BF16), pltpu.SemaphoreType.DMA((5,))],
        **small(2),
    )(core, *[pltpu.with_memory_space_constraint(array, pltpu.HBM) for array in (orbitals, gauge)])


def correlate(meta, base, directions, cosines, sines, own, sources):
    nb = (own[0].shape[1] - PACKED_ROWS) // 2
    points = own[0].shape[2]

    def body(meta, cosines, sines, front, rear, *refs):
        sources_in = refs[:2]
        give, keep, left, phased = refs[2:]
        for p in range(4):
            slot, k = meta[0, base + p], meta[1, base + p]
            source = sources_in[p % 2]
            lefts, shifted = left.at[p % 2], phased.at[p % 2]
            for half, ref in enumerate((front, rear)):

                @pl.when(k // 2 == half)
                def _():
                    start = pl.multiple_of((k - 2 * half) * nb, nb)
                    for c in range(2):
                        lefts[c * nb : (c + 1) * nb, :] = ref[c, pl.ds(start, nb), :]

            row = directions[p % 2] * 4 + k
            cosine = cosines[pl.ds(row, 1), :]
            sine = sines[pl.ds(row, 1), :]
            start = pl.multiple_of(slot * nb, nb)
            source_re = source[0, pl.ds(start, nb), :].astype(F32)
            source_im = source[1, pl.ds(start, nb), :].astype(F32)
            shifted[0:nb, :] = (cosine * source_re + sine * source_im).astype(BF16)
            shifted[nb:, :] = (cosine * source_im - sine * source_re).astype(BF16)
            full = lax.dot_general(lefts[...], shifted[...], CONTRACT_LAST, preferred_element_type=F32)
            out = give if p < 2 else keep
            out[p % 2, 0] = full[:nb, :nb] + full[nb:, nb:]
            out[p % 2, 1] = full[:nb, nb:] - full[nb:, :nb]

    half_out = VMEM((2, 2, nb, nb), F32)
    return pl.pallas_call(
        body,
        name="correlate",
        out_shape=(half_out, half_out),
        in_specs=specs(pltpu.SMEM, *[VMEM] * 6),
        out_specs=tuple(specs(VMEM, VMEM)),
        scratch_shapes=[VMEM((2, 2 * nb, points), BF16), VMEM((2, 2 * nb, points), BF16)],
        **small(8),
    )(meta, *vmem(cosines, sines, *own, *sources))


def split_parts(values):
    high = values.astype(BF16)
    low = (values - high.astype(F32)).astype(BF16)
    return high, low


def rotate_pair(raw_parts, left, right):
    nb = left[0].shape[0]
    raw_re, raw_im = [jnp.concatenate(split_parts(part), axis=1) for part in raw_parts]
    raw = jnp.concatenate([raw_re, raw_im], axis=0)
    wide = jnp.concatenate(right, axis=1)
    prod = jnp.dot(raw, jnp.concatenate([wide, wide], axis=0), preferred_element_type=F32)
    temp_re = prod[:nb, :nb] - prod[nb:, nb:]
    temp_im = prod[:nb, nb:] + prod[nb:, :nb]
    re_high, re_low = split_parts(temp_re)
    im_high, im_low = split_parts(temp_im)
    temp = jnp.concatenate(
        [jnp.concatenate([re_high, im_high], axis=1), jnp.concatenate([re_low, im_low], axis=1)], axis=0
    )
    tall = jnp.concatenate(left, axis=1)
    prod = lax.dot_general(
        jnp.concatenate([tall, tall], axis=0), temp, CONTRACT_FIRST, preferred_element_type=F32
    )
    return prod[:nb, :nb] + prod[nb:, nb:], prod[:nb, nb:] - prod[nb:, :nb]


def encode(chip):
    pairs, _, nb, _ = chip.shape
    largest = jnp.max(jnp.abs(chip), axis=(1, 2, 3))
    exponent = jnp.floor(jnp.log2(jnp.maximum(largest, F32(1e-30))))
    scaled = chip * jnp.exp2(F32(SHIFT) - exponent)[:, None, None, None]
    tail = jnp.broadcast_to(exponent[:, None, None], (pairs, 8, nb))
    coded = jnp.concatenate([scaled.reshape(pairs, 2 * nb, nb), tail], axis=1).astype(jnp.float16)
    return lax.optimization_barrier(coded)


def decode(coded):
    pairs, rows, nb = coded.shape
    exponent = coded[:, rows - 1, 0].astype(F32)
    values = coded[:, : 2 * nb].astype(F32) * jnp.exp2(exponent - F32(SHIFT))[:, None, None]
    return values.reshape(pairs, 2, nb, nb)


def rotate(meta, columns, raw, gauge, packed, right_of, layout):
    nb = gauge.shape[2]
    pairs = len(right_of)

    def unpack(ref, c):
        rows = ref.shape[1] - PACKED_ROWS
        blocks = [ref[c, rows:, j * nb : (j + 1) * nb] for j in range(ref.shape[2] // nb)]
        return jnp.concatenate(blocks, axis=0)

    def body(slots, raw, gauge, *refs):
        payloads, outs = refs[: len(packed)], refs[len(packed) :]
        for p in range(pairs):
            k = slots[1, columns[p]]
            if right_of[p] is None:
                right = [gauge[c, slots[3, columns[p]]] for c in range(2)]
            else:
                right = [unpack(payloads[right_of[p]], c) for c in range(2)]
            out_re, out_im = rotate_pair([raw[p, c] for c in range(2)], [gauge[c, k] for c in range(2)], right)
            for out, rows in zip(outs, layout):
                for row, (pair, adjoint) in enumerate(rows):
                    if pair == p and adjoint:
                        out[row, 0] = out_re.T
                        out[row, 1] = -out_im.T
                    elif pair == p:
                        out[row, 0] = out_re
                        out[row, 1] = out_im

    return pl.pallas_call(
        body,
        name="rotate",
        out_shape=tuple(VMEM((len(rows), 2, nb, nb), F32) for rows in layout),
        in_specs=specs(pltpu.SMEM, *[VMEM] * (2 + len(packed))),
        out_specs=tuple(specs(*[VMEM] * len(layout))),
        **small(8),
    )(meta, *vmem(raw, gauge, *packed))


def place(targets, meta, blocks, outs):
    nb = blocks[0].shape[-1]
    shape = jax.ShapeDtypeStruct((3, 2, 4, nb, nb), F32)
    previous = () if outs is None else tuple(outs)
    def body(slots, *refs):
        sems = refs[-1]
        into = refs[-3:-1]
        copies = []
        for block, rows in zip(refs, targets):
            for n, (output, direction, column) in enumerate(rows):
                target = into[output].at[direction, :, slots[3 if output else 1, column]]
                copies.append(pltpu.make_async_copy(block.at[n], target, sems.at[len(copies)]))
        for copy in copies:
            copy.start()
        for copy in copies:
            copy.wait()

    count = len(blocks)
    total = sum(len(rows) for rows in targets)
    return pl.pallas_call(
        body,
        out_shape=(shape, shape),
        name="place",
        in_specs=specs(pltpu.SMEM, *[VMEM] * count, *[pl.ANY] * len(previous)),
        out_specs=tuple(specs(pl.ANY, pl.ANY)),
        scratch_shapes=[pltpu.SemaphoreType.DMA((total,))],
        input_output_aliases={1 + count: 0, 2 + count: 1} if previous else {},
        **small(2),
    )(meta, *vmem(*blocks), *previous)


def shards(orbitals, gauge, neighbour, wrap_shift):
    kloc = orbitals.shape[1]
    grid_points = orbitals.shape[3]
    ka_count = lax.axis_size("ka")
    ga_count = lax.axis_size("ga")
    device = lax.axis_index("ka")
    grid_part = lax.axis_index("ga")
    core = grid_part % 2
    plane_count = grid_points // (GY * GZ)
    counts = (kloc, KRING, ka_count // KRING)

    ring_back = [(d, d // KRING * KRING + (d - 1) % KRING) for d in range(ka_count)]
    outer_back = [(d, (d - KRING) % ka_count) for d in range(ka_count)]
    ring_ahead = [(t, s) for s, t in ring_back]
    outer_ahead = [(t, s) for s, t in outer_back]
    sibling = [(g, g ^ 1) for g in range(ga_count)]
    across = [(g, g ^ 2) for g in range(ga_count)]

    core_index = core.reshape(1).astype(jnp.int32)
    front = load(core_index, orbitals, gauge, 0)
    beyond_front = lax.ppermute(front, "ka", outer_back)
    beside_front = lax.ppermute(front, "ka", ring_back)
    rear = load(core_index, orbitals, gauge, 1)
    beyond_rear = lax.ppermute(rear, "ka", outer_back)
    beside_rear = lax.ppermute(rear, "ka", ring_back)
    own = (front, rear)

    fractions = grid_fractions(grid_part * plane_count, plane_count, plane_count * ga_count)
    my_table = lax.dynamic_slice_in_dim(neighbour, device * kloc, kloc, 0) % kloc
    my_shift = lax.dynamic_slice_in_dim(wrap_shift, device * kloc, kloc, 0)
    slots = jnp.arange(kloc, dtype=jnp.int32)
    local = jnp.stack([1 - core, 1 - core, core, core]).astype(jnp.int32)
    is_second = slots % 2

    def k_slots(direction, wanted):
        match = my_table[:, direction][:, None] == wanted[None, :]
        return jnp.sum(jnp.where(match, slots[:, None], 0), axis=0)

    order = local + 2 * is_second
    first_k = jnp.stack([k_slots(0, order), k_slots(1, local), k_slots(1, local + 2)])
    second_k = jnp.stack([k_slots(0, order), k_slots(2, local), k_slots(2, local + 2)])
    ks = jnp.where(is_second == 0, first_k, second_k).reshape(-1)
    locals_ = jnp.tile(local, 3)
    meta = jnp.stack([locals_, ks, locals_, jnp.concatenate([order, local, local + 2])])

    angles = jnp.concatenate([phase_angles(my_shift[:, b, :], b, counts, fractions) for b in range(3)])
    cosines, sines = jnp.cos(angles), jnp.sin(angles)

    give, keep = correlate(meta, 0, (0, 0), cosines, sines, own, own)
    got = lax.ppermute(give, "ga", sibling)
    give_front, keep_front = correlate(meta, 4, (1, 2), cosines, sines, own, (beside_front, beyond_front))
    got_front = lax.ppermute(give_front, "ga", sibling)
    coded = encode(jnp.concatenate([keep + got, keep_front + got_front], axis=0))
    coded, beside_rear, beyond_rear = lax.optimization_barrier((coded, beside_rear, beyond_rear))
    other = lax.ppermute(coded, "ga", across)
    give, keep = correlate(meta, 8, (1, 2), cosines, sines, own, (beside_rear, beyond_rear))
    coded_rear = encode(keep + lax.ppermute(give, "ga", sibling))
    other_rear = lax.ppermute(coded_rear, "ga", across)

    other, coded_rear = lax.optimization_barrier((other, coded_rear))
    first, adj_x, adj_y = rotate(
        meta, (2, 3, 6, 7), decode(coded) + decode(other), gauge, (beside_front, beyond_front), (None, None, 0, 1),
        [[(0, 0), (1, 0), (2, 0), (3, 0), (0, 1), (1, 1)], [(2, 1)], [(3, 1)]],
    )
    last, adj_x_rear, adj_y_rear = rotate(
        meta, (10, 11), decode(coded_rear) + decode(other_rear), gauge, (beside_rear, beyond_rear), (0, 1),
        [[(0, 0), (1, 0)], [(0, 1)], [(1, 1)]],
    )
    adj_y = lax.ppermute(jnp.concatenate([adj_y, adj_y_rear], axis=0), "ka", outer_ahead)
    adj_x = lax.ppermute(jnp.concatenate([adj_x, adj_x_rear], axis=0), "ka", ring_ahead)
    fwd = jnp.concatenate([first, last], axis=0)
    fwd_sib = lax.ppermute(fwd, "ga", sibling)
    adj = jnp.concatenate([adj_x, adj_y], axis=0)
    adj_sib = lax.ppermute(adj, "ga", sibling)
    targets = [
        [(0, 0, i), (0, 0, i + 1), (0, 1, i + 4), (0, 2, i + 5), (1, 0, i), (1, 0, i + 1), (0, 1, i + 8), (0, 2, i + 9)]
        for i in (2, 0)
    ]
    outs = place(targets, meta, (fwd, fwd_sib), None)
    targets = [[(1, 1, i + 4), (1, 1, i + 8), (1, 2, i + 5), (1, 2, i + 9)] for i in (2, 0)]
    return tuple(place(targets, meta, (adj, adj_sib), outs))


def solution(mesh):
    in_specs = (P(None, "ka", None, "ga"), P(None, "ka", None, None), P(), P())
    out_specs = (P(None, None, "ka", None, None), P(None, None, "ka", None, None))
    return jax.shard_map(shards, mesh=mesh, in_specs=in_specs, out_specs=out_specs, check_vma=False)
```

```python
import math

import jax
import jax.numpy as jnp
from jax import lax
from jax.experimental import pallas as pl
from jax.experimental.pallas import tpu as pltpu
from jax.sharding import PartitionSpec as P

KRING = 4
GY = 32
GZ = 32
F32 = jnp.float32
BF16 = jnp.bfloat16
PACKED_ROWS = 16
SHIFT = 13
VMEM = pltpu.VMEM
CONTRACT_LAST = (((1,), (1,)), ((), ()))
CONTRACT_FIRST = (((0,), (0,)), ((), ()))


def grid_fractions(plane_first, plane_count, plane_total):
    point_index = jnp.arange(plane_count * GY * GZ, dtype=jnp.int32)
    plane = point_index // (GY * GZ) + plane_first
    middle = point_index // GZ % GY
    inner = point_index % GZ
    return [
        plane.astype(F32) / F32(plane_total),
        middle.astype(F32) / F32(GY),
        inner.astype(F32) / F32(GZ),
    ]


def phase_angles(shift_rows, direction, mesh_counts, fractions):
    total = jnp.zeros((shift_rows.shape[0], fractions[0].shape[0]), F32)
    for lattice in range(3):
        step = 1.0 / mesh_counts[lattice] if lattice == direction else 0.0
        wave = shift_rows[:, lattice].astype(F32) + F32(step)
        total = total + wave[:, None] * fractions[lattice][None, :]
    return F32(2.0 * math.pi) * total


def vmem(*arrays):
    return tuple(pltpu.with_memory_space_constraint(array, VMEM) for array in arrays)


def specs(*spaces):
    return [pl.BlockSpec(memory_space=space) for space in spaces]


def small(mib):
    return {
        "cost_estimate": pl.CostEstimate(flops=1, bytes_accessed=1, transcendentals=0),
        "compiler_params": pltpu.CompilerParams(vmem_limit_bytes=mib * 2**20),
    }


def load(core, orbitals, gauge, part):
    nb, points = orbitals.shape[2:]
    blocks = points // nb

    def body(core, orbitals, gauge, out, block, sems):
        copies = [
            pltpu.make_async_copy(
                orbitals.at[c, 2 * part + slot], out.at[c, slot * nb : (slot + 1) * nb], sems.at[2 * c + slot]
            )
            for c in range(2)
            for slot in range(2)
        ]
        copies.append(pltpu.make_async_copy(gauge.at[:, 2 * part + core[0]], block, sems.at[4]))
        for copy in copies:
            copy.start()
        copies[4].wait()
        for c in range(2):
            for j in range(blocks):
                rows = block[c, j * PACKED_ROWS : (j + 1) * PACKED_ROWS, :]
                out[c, 2 * nb :, j * nb : (j + 1) * nb] = rows
        for copy in copies[:4]:
            copy.wait()

    return pl.pallas_call(
        body,
        name="load",
        out_shape=VMEM((2, 2 * nb + PACKED_ROWS, points), BF16),
        in_specs=specs(pltpu.SMEM, pl.ANY, pl.ANY),
        out_specs=specs(VMEM)[0],
        scratch_shapes=[VMEM((2, nb, nb), BF16), pltpu.SemaphoreType.DMA((5,))],
        **small(2),
    )(core, *[pltpu.with_memory_space_constraint(array, pltpu.HBM) for array in (orbitals, gauge)])


def correlate(meta, base, directions, cosines, sines, own, sources):
    nb = (own[0].shape[1] - PACKED_ROWS) // 2
    points = own[0].shape[2]

    def body(meta, cosines, sines, front, rear, first, second, out, arrived, left, phased, sems):
        copies = []
        for p, source in enumerate((first, second)):
            rows = pl.ds(pl.multiple_of(meta[0, base + p] * nb, nb), nb)
            copies += [pltpu.make_async_copy(source.at[c, rows], arrived.at[p, c], sems.at[p, c]) for c in range(2)]
        for copy in copies:
            copy.start()
        for p in range(2):
            k = meta[1, base + p]
            lefts, shifted = left.at[p], phased.at[p]
            for half, ref in enumerate((front, rear)):

                @pl.when(k // 2 == half)
                def _():
                    start = pl.multiple_of((k - 2 * half) * nb, nb)
                    for c in range(2):
                        lefts[c * nb : (c + 1) * nb, :] = ref[c, pl.ds(start, nb), :]

            row = directions[p] * 4 + k
            cosine = cosines[pl.ds(row, 1), :]
            sine = sines[pl.ds(row, 1), :]
            for c in range(2):
                copies[2 * p + c].wait()
            source_re = arrived[p, 0].astype(F32)
            source_im = arrived[p, 1].astype(F32)
            shifted[0:nb, :] = (cosine * source_re + sine * source_im).astype(BF16)
            shifted[nb:, :] = (cosine * source_im - sine * source_re).astype(BF16)
            full = lax.dot_general(lefts[...], shifted[...], CONTRACT_LAST, preferred_element_type=F32)
            out[p, 0] = full[:nb, :nb] + full[nb:, nb:]
            out[p, 1] = full[:nb, nb:] - full[nb:, :nb]

    return pl.pallas_call(
        body,
        name="correlate",
        out_shape=VMEM((2, 2, nb, nb), F32),
        in_specs=specs(pltpu.SMEM, *[VMEM] * 4, pl.ANY, pl.ANY),
        out_specs=specs(VMEM)[0],
        scratch_shapes=[
            VMEM((2, 2, nb, points), BF16),
            VMEM((2, 2 * nb, points), BF16),
            VMEM((2, 2 * nb, points), BF16),
            pltpu.SemaphoreType.DMA((2, 2)),
        ],
        **small(8),
    )(meta, *vmem(cosines, sines, *own), *sources)


def split_parts(values):
    high = values.astype(BF16)
    low = (values - high.astype(F32)).astype(BF16)
    return high, low


def rotate_pair(raw_parts, left, right):
    nb = left[0].shape[0]
    raw_re, raw_im = [jnp.concatenate(split_parts(part), axis=1) for part in raw_parts]
    raw = jnp.concatenate([raw_re, raw_im], axis=0)
    wide = jnp.concatenate(right, axis=1)
    prod = jnp.dot(raw, jnp.concatenate([wide, wide], axis=0), preferred_element_type=F32)
    temp_re = prod[:nb, :nb] - prod[nb:, nb:]
    temp_im = prod[:nb, nb:] + prod[nb:, :nb]
    re_high, re_low = split_parts(temp_re)
    im_high, im_low = split_parts(temp_im)
    temp = jnp.concatenate(
        [jnp.concatenate([re_high, im_high], axis=1), jnp.concatenate([re_low, im_low], axis=1)], axis=0
    )
    tall = jnp.concatenate(left, axis=1)
    prod = lax.dot_general(
        jnp.concatenate([tall, tall], axis=0), temp, CONTRACT_FIRST, preferred_element_type=F32
    )
    return prod[:nb, :nb] + prod[nb:, nb:], prod[:nb, nb:] - prod[nb:, :nb]


def encode(chip):
    pairs, _, nb, _ = chip.shape
    largest = jnp.max(jnp.abs(chip), axis=(1, 2, 3))
    exponent = jnp.floor(jnp.log2(jnp.maximum(largest, F32(1e-30))))
    scaled = chip * jnp.exp2(F32(SHIFT) - exponent)[:, None, None, None]
    tail = jnp.broadcast_to(exponent[:, None, None], (pairs, 8, nb))
    coded = jnp.concatenate([scaled.reshape(pairs, 2 * nb, nb), tail], axis=1).astype(jnp.float16)
    return lax.optimization_barrier(coded)


def decode(coded):
    pairs, rows, nb = coded.shape
    exponent = coded[:, rows - 1, 0].astype(F32)
    values = coded[:, : 2 * nb].astype(F32) * jnp.exp2(exponent - F32(SHIFT))[:, None, None]
    return values.reshape(pairs, 2, nb, nb)


def rotate(meta, columns, raw, gauge, packed, right_of, layout):
    nb = gauge.shape[2]
    pairs = len(right_of)

    def unpack(ref, c):
        rows = ref.shape[1] - PACKED_ROWS
        blocks = [ref[c, rows:, j * nb : (j + 1) * nb] for j in range(ref.shape[2] // nb)]
        return jnp.concatenate(blocks, axis=0)

    def body(slots, raw, gauge, *refs):
        payloads, outs = refs[: len(packed)], refs[len(packed) :]
        for p in range(pairs):
            k = slots[1, columns[p]]
            if right_of[p] is None:
                right = [gauge[c, slots[3, columns[p]]] for c in range(2)]
            else:
                right = [unpack(payloads[right_of[p]], c) for c in range(2)]
            out_re, out_im = rotate_pair([raw[p, c] for c in range(2)], [gauge[c, k] for c in range(2)], right)
            for out, rows in zip(outs, layout):
                for row, (pair, adjoint) in enumerate(rows):
                    if pair == p and adjoint:
                        out[row, 0] = out_re.T
                        out[row, 1] = -out_im.T
                    elif pair == p:
                        out[row, 0] = out_re
                        out[row, 1] = out_im

    return pl.pallas_call(
        body,
        name="rotate",
        out_shape=tuple(VMEM((len(rows), 2, nb, nb), F32) for rows in layout),
        in_specs=specs(pltpu.SMEM, *[VMEM] * (2 + len(packed))),
        out_specs=tuple(specs(*[VMEM] * len(layout))),
        **small(8),
    )(meta, *vmem(raw, gauge, *packed))


def place(targets, meta, blocks, outs):
    nb = blocks[0].shape[-1]
    shape = jax.ShapeDtypeStruct((3, 2, 4, nb, nb), F32)
    previous = () if outs is None else tuple(outs)
    def body(slots, *refs):
        sems = refs[-1]
        into = refs[-3:-1]
        copies = []
        for block, rows in zip(refs, targets):
            for n, (output, direction, column) in enumerate(rows):
                target = into[output].at[direction, :, slots[3 if output else 1, column]]
                copies.append(pltpu.make_async_copy(block.at[n], target, sems.at[len(copies)]))
        for copy in copies:
            copy.start()
        for copy in copies:
            copy.wait()

    count = len(blocks)
    total = sum(len(rows) for rows in targets)
    return pl.pallas_call(
        body,
        out_shape=(shape, shape),
        name="place",
        in_specs=specs(pltpu.SMEM, *[VMEM] * count, *[pl.ANY] * len(previous)),
        out_specs=tuple(specs(pl.ANY, pl.ANY)),
        scratch_shapes=[pltpu.SemaphoreType.DMA((total,))],
        input_output_aliases={1 + count: 0, 2 + count: 1} if previous else {},
        **small(2),
    )(meta, *vmem(*blocks), *previous)


def shards(orbitals, gauge, neighbour, wrap_shift):
    kloc = orbitals.shape[1]
    grid_points = orbitals.shape[3]
    ka_count = lax.axis_size("ka")
    ga_count = lax.axis_size("ga")
    device = lax.axis_index("ka")
    grid_part = lax.axis_index("ga")
    core = grid_part % 2
    plane_count = grid_points // (GY * GZ)
    counts = (kloc, KRING, ka_count // KRING)

    ring_back = [(d, d // KRING * KRING + (d - 1) % KRING) for d in range(ka_count)]
    outer_back = [(d, (d - KRING) % ka_count) for d in range(ka_count)]
    ring_ahead = [(t, s) for s, t in ring_back]
    outer_ahead = [(t, s) for s, t in outer_back]
    sibling = [(g, g ^ 1) for g in range(ga_count)]
    across = [(g, g ^ 2) for g in range(ga_count)]

    core_index = core.reshape(1).astype(jnp.int32)
    front = load(core_index, orbitals, gauge, 0)
    beyond_front = lax.ppermute(front, "ka", outer_back)
    beside_front = lax.ppermute(front, "ka", ring_back)
    rear = load(core_index, orbitals, gauge, 1)
    beyond_rear = lax.ppermute(rear, "ka", outer_back)
    beside_rear = lax.ppermute(rear, "ka", ring_back)
    own = (front, rear)

    fractions = grid_fractions(grid_part * plane_count, plane_count, plane_count * ga_count)
    my_table = lax.dynamic_slice_in_dim(neighbour, device * kloc, kloc, 0) % kloc
    my_shift = lax.dynamic_slice_in_dim(wrap_shift, device * kloc, kloc, 0)
    slots = jnp.arange(kloc, dtype=jnp.int32)
    local = jnp.stack([1 - core, 1 - core, core, core]).astype(jnp.int32)
    is_second = slots % 2

    def k_slots(direction, wanted):
        match = my_table[:, direction][:, None] == wanted[None, :]
        return jnp.sum(jnp.where(match, slots[:, None], 0), axis=0)

    order = local + 2 * is_second
    first_k = jnp.stack([k_slots(0, order), k_slots(1, local), k_slots(1, local + 2)])
    second_k = jnp.stack([k_slots(0, order), k_slots(2, local), k_slots(2, local + 2)])
    ks = jnp.where(is_second == 0, first_k, second_k).reshape(-1)
    locals_ = jnp.tile(local, 3)
    meta = jnp.stack([locals_, ks, locals_, jnp.concatenate([order, local, local + 2])])

    angles = jnp.concatenate([phase_angles(my_shift[:, b, :], b, counts, fractions) for b in range(3)])
    cosines, sines = jnp.cos(angles), jnp.sin(angles)

    def halves(base, directions, sources):
        give = correlate(meta, base, directions, cosines, sines, own, sources)
        got = lax.ppermute(give, "ga", sibling)
        return got, correlate(meta, base + 2, directions, cosines, sines, own, sources)

    got, keep = halves(0, (0, 0), own)
    got_front, keep_front = halves(4, (1, 2), (beside_front, beyond_front))
    coded = encode(jnp.concatenate([keep + got, keep_front + got_front], axis=0))
    other = lax.ppermute(coded, "ga", across)
    coded, beside_rear, beyond_rear = lax.optimization_barrier((coded, beside_rear, beyond_rear))
    got, keep = halves(8, (1, 2), (beside_rear, beyond_rear))
    other, got = lax.optimization_barrier((other, got))
    coded_rear = encode(keep + got)
    other_rear = lax.ppermute(coded_rear, "ga", across)

    first, adj_x, adj_y = rotate(
        meta, (2, 3, 6, 7), decode(coded) + decode(other), gauge, (beside_front, beyond_front), (None, None, 0, 1),
        [[(0, 0), (1, 0), (2, 0), (3, 0), (0, 1), (1, 1)], [(2, 1)], [(3, 1)]],
    )
    last, adj_x_rear, adj_y_rear = rotate(
        meta, (10, 11), decode(coded_rear) + decode(other_rear), gauge, (beside_rear, beyond_rear), (0, 1),
        [[(0, 0), (1, 0)], [(0, 1)], [(1, 1)]],
    )
    adj_y = lax.ppermute(encode(jnp.concatenate([adj_y, adj_y_rear], axis=0)), "ka", outer_ahead)
    adj_x = lax.ppermute(encode(jnp.concatenate([adj_x, adj_x_rear], axis=0)), "ka", ring_ahead)
    fwd = jnp.concatenate([first, last], axis=0)
    fwd_sib = lax.ppermute(fwd, "ga", sibling)
    adj = lax.optimization_barrier(jnp.concatenate([adj_x, adj_y], axis=0))
    adj_sib = lax.ppermute(adj, "ga", sibling)
    targets = [
        [(0, 0, i), (0, 0, i + 1), (0, 1, i + 4), (0, 2, i + 5), (1, 0, i), (1, 0, i + 1), (0, 1, i + 8), (0, 2, i + 9)]
        for i in (2, 0)
    ]
    outs = place(targets, meta, (fwd, fwd_sib), None)
    adj_sib, *outs = lax.optimization_barrier((adj_sib, *outs))
    adj, adj_sib = decode(adj), decode(adj_sib)
    targets = [[(1, 1, i + 4), (1, 1, i + 8), (1, 2, i + 5), (1, 2, i + 9)] for i in (2, 0)]
    return tuple(place(targets, meta, (adj, adj_sib), outs))


def solution(mesh):
    in_specs = (P(None, "ka", None, "ga"), P(None, "ka", None, None), P(), P())
    out_specs = (P(None, None, "ka", None, None), P(None, None, "ka", None, None))
    return jax.shard_map(shards, mesh=mesh, in_specs=in_specs, out_specs=out_specs, check_vma=False)
```

```python
import math

import jax
import jax.numpy as jnp
from jax import lax
from jax.experimental import pallas as pl
from jax.experimental.pallas import tpu as pltpu
from jax.sharding import PartitionSpec as P

KRING = 4
GY = 32
GZ = 32
F32 = jnp.float32
BF16 = jnp.bfloat16
SHIFT = 13
VMEM = pltpu.VMEM
CONTRACT_LAST = (((1,), (1,)), ((), ()))
CONTRACT_FIRST = (((0,), (0,)), ((), ()))


def grid_fractions(plane_first, plane_count, plane_total):
    point_index = jnp.arange(plane_count * GY * GZ, dtype=jnp.int32)
    plane = point_index // (GY * GZ) + plane_first
    middle = point_index // GZ % GY
    inner = point_index % GZ
    return [
        plane.astype(F32) / F32(plane_total),
        middle.astype(F32) / F32(GY),
        inner.astype(F32) / F32(GZ),
    ]


def phase_angles(shift_rows, direction, mesh_counts, fractions):
    total = jnp.zeros((shift_rows.shape[0], fractions[0].shape[0]), F32)
    for lattice in range(3):
        step = 1.0 / mesh_counts[lattice] if lattice == direction else 0.0
        wave = shift_rows[:, lattice].astype(F32) + F32(step)
        total = total + wave[:, None] * fractions[lattice][None, :]
    return F32(2.0 * math.pi) * total


def vmem(*arrays):
    return tuple(pltpu.with_memory_space_constraint(array, VMEM) for array in arrays)


def specs(*spaces):
    return [pl.BlockSpec(memory_space=space) for space in spaces]


def small(mib):
    return {
        "cost_estimate": pl.CostEstimate(flops=1, bytes_accessed=1, transcendentals=0),
        "compiler_params": pltpu.CompilerParams(vmem_limit_bytes=mib * 2**20),
    }


def load(orbitals, part):
    nb, points = orbitals.shape[2:]

    def body(orbitals, out, sems):
        copies = [
            pltpu.make_async_copy(
                orbitals.at[c, 2 * part + slot], out.at[c, slot * nb : (slot + 1) * nb], sems.at[2 * c + slot]
            )
            for c in range(2)
            for slot in range(2)
        ]
        for copy in copies:
            copy.start()
        for copy in copies:
            copy.wait()

    return pl.pallas_call(
        body,
        name="load",
        out_shape=VMEM((2, 2 * nb, points), BF16),
        in_specs=specs(pl.ANY),
        out_specs=specs(VMEM)[0],
        scratch_shapes=[pltpu.SemaphoreType.DMA((4,))],
        **small(2),
    )(pltpu.with_memory_space_constraint(orbitals, pltpu.HBM))


def correlate(meta, base, directions, cosines, sines, own, sources):
    nb = own[0].shape[1] // 2
    points = own[0].shape[2]

    def body(meta, cosines, sines, front, rear, first, second, out, arrived, left, phased, sems):
        copies = []
        for p, source in enumerate((first, second)):
            rows = pl.ds(pl.multiple_of(meta[0, base + p] * nb, nb), nb)
            copies += [pltpu.make_async_copy(source.at[c, rows], arrived.at[p, c], sems.at[p, c]) for c in range(2)]
        for copy in copies:
            copy.start()
        for p in range(2):
            k = meta[1, base + p]
            lefts, shifted = left.at[p], phased.at[p]
            for half, ref in enumerate((front, rear)):

                @pl.when(k // 2 == half)
                def _():
                    start = pl.multiple_of((k - 2 * half) * nb, nb)
                    for c in range(2):
                        lefts[c * nb : (c + 1) * nb, :] = ref[c, pl.ds(start, nb), :]

            row = directions[p] * 4 + k
            cosine = cosines[pl.ds(row, 1), :]
            sine = sines[pl.ds(row, 1), :]
            for c in range(2):
                copies[2 * p + c].wait()
            source_re = arrived[p, 0].astype(F32)
            source_im = arrived[p, 1].astype(F32)
            shifted[0:nb, :] = (cosine * source_re + sine * source_im).astype(BF16)
            shifted[nb:, :] = (cosine * source_im - sine * source_re).astype(BF16)
            full = lax.dot_general(lefts[...], shifted[...], CONTRACT_LAST, preferred_element_type=F32)
            out[p, 0] = full[:nb, :nb] + full[nb:, nb:]
            out[p, 1] = full[:nb, nb:] - full[nb:, :nb]

    return pl.pallas_call(
        body,
        name="correlate",
        out_shape=VMEM((2, 2, nb, nb), F32),
        in_specs=specs(pltpu.SMEM, *[VMEM] * 4, pl.ANY, pl.ANY),
        out_specs=specs(VMEM)[0],
        scratch_shapes=[
            VMEM((2, 2, nb, points), BF16),
            VMEM((2, 2 * nb, points), BF16),
            VMEM((2, 2 * nb, points), BF16),
            pltpu.SemaphoreType.DMA((2, 2)),
        ],
        **small(8),
    )(meta, *vmem(cosines, sines, *own), *sources)


def split_parts(values):
    high = values.astype(BF16)
    low = (values - high.astype(F32)).astype(BF16)
    return high, low


def rotate_pair(raw_parts, left, right):
    nb = left[0].shape[0]
    raw_re, raw_im = [jnp.concatenate(split_parts(part), axis=1) for part in raw_parts]
    raw = jnp.concatenate([raw_re, raw_im], axis=0)
    wide = jnp.concatenate(right, axis=1)
    prod = jnp.dot(raw, jnp.concatenate([wide, wide], axis=0), preferred_element_type=F32)
    temp_re = prod[:nb, :nb] - prod[nb:, nb:]
    temp_im = prod[:nb, nb:] + prod[nb:, :nb]
    re_high, re_low = split_parts(temp_re)
    im_high, im_low = split_parts(temp_im)
    temp = jnp.concatenate(
        [jnp.concatenate([re_high, im_high], axis=1), jnp.concatenate([re_low, im_low], axis=1)], axis=0
    )
    tall = jnp.concatenate(left, axis=1)
    prod = lax.dot_general(
        jnp.concatenate([tall, tall], axis=0), temp, CONTRACT_FIRST, preferred_element_type=F32
    )
    return prod[:nb, :nb] + prod[nb:, nb:], prod[:nb, nb:] - prod[nb:, :nb]


def encode(chip):
    pairs, _, nb, _ = chip.shape
    largest = jnp.max(jnp.abs(chip), axis=(1, 2, 3))
    exponent = jnp.floor(jnp.log2(jnp.maximum(largest, F32(1e-30))))
    scaled = chip * jnp.exp2(F32(SHIFT) - exponent)[:, None, None, None]
    tail = jnp.broadcast_to(exponent[:, None, None], (pairs, 8, nb))
    coded = jnp.concatenate([scaled.reshape(pairs, 2 * nb, nb), tail], axis=1).astype(jnp.float16)
    return lax.optimization_barrier(coded)


def decode(coded):
    pairs, rows, nb = coded.shape
    exponent = coded[:, rows - 1, 0].astype(F32)
    values = coded[:, : 2 * nb].astype(F32) * jnp.exp2(exponent - F32(SHIFT))[:, None, None]
    return values.reshape(pairs, 2, nb, nb)


def rotate(meta, columns, raw, gauge, packed, right_of, layout):
    nb = gauge.shape[2]
    pairs = len(right_of)

    def body(slots, raw, gauge, *refs):
        payloads, outs = refs[: len(packed)], refs[len(packed) :]
        for p in range(pairs):
            k = slots[1, columns[p]]
            if right_of[p] is None:
                right = [gauge[c, slots[3, columns[p]]] for c in range(2)]
            else:
                right = [payloads[right_of[p][0]][c, right_of[p][1]] for c in range(2)]
            out_re, out_im = rotate_pair([raw[p, c] for c in range(2)], [gauge[c, k] for c in range(2)], right)
            for out, rows in zip(outs, layout):
                for row, (pair, adjoint) in enumerate(rows):
                    if pair == p and adjoint:
                        out[row, 0] = out_re.T
                        out[row, 1] = -out_im.T
                    elif pair == p:
                        out[row, 0] = out_re
                        out[row, 1] = out_im

    return pl.pallas_call(
        body,
        name="rotate",
        out_shape=tuple(VMEM((len(rows), 2, nb, nb), F32) for rows in layout),
        in_specs=specs(pltpu.SMEM, *[VMEM] * (2 + len(packed))),
        out_specs=tuple(specs(*[VMEM] * len(layout))),
        **small(8),
    )(meta, *vmem(raw, gauge, *packed))


def place(targets, meta, blocks, outs):
    nb = blocks[0].shape[-1]
    shape = jax.ShapeDtypeStruct((3, 2, 4, nb, nb), F32)
    previous = () if outs is None else tuple(outs)
    def body(slots, *refs):
        sems = refs[-1]
        into = refs[-3:-1]
        copies = []
        for block, rows in zip(refs, targets):
            for n, (output, direction, column) in enumerate(rows):
                target = into[output].at[direction, :, slots[3 if output else 1, column]]
                copies.append(pltpu.make_async_copy(block.at[n], target, sems.at[len(copies)]))
        for copy in copies:
            copy.start()
        for copy in copies:
            copy.wait()

    count = len(blocks)
    total = sum(len(rows) for rows in targets)
    return pl.pallas_call(
        body,
        out_shape=(shape, shape),
        name="place",
        in_specs=specs(pltpu.SMEM, *[VMEM] * count, *[pl.ANY] * len(previous)),
        out_specs=tuple(specs(pl.ANY, pl.ANY)),
        scratch_shapes=[pltpu.SemaphoreType.DMA((total,))],
        input_output_aliases={1 + count: 0, 2 + count: 1} if previous else {},
        **small(2),
    )(meta, *vmem(*blocks), *previous)


def shards(orbitals, gauge, neighbour, wrap_shift):
    kloc = orbitals.shape[1]
    grid_points = orbitals.shape[3]
    ka_count = lax.axis_size("ka")
    ga_count = lax.axis_size("ga")
    device = lax.axis_index("ka")
    grid_part = lax.axis_index("ga")
    core = grid_part % 2
    plane_count = grid_points // (GY * GZ)
    counts = (kloc, KRING, ka_count // KRING)

    ring_back = [(d, d // KRING * KRING + (d - 1) % KRING) for d in range(ka_count)]
    outer_back = [(d, (d - KRING) % ka_count) for d in range(ka_count)]
    ring_ahead = [(t, s) for s, t in ring_back]
    outer_ahead = [(t, s) for s, t in outer_back]
    sibling = [(g, g ^ 1) for g in range(ga_count)]
    across = [(g, g ^ 2) for g in range(ga_count)]

    nb = orbitals.shape[2]
    front = load(orbitals, 0)
    beyond_front = lax.ppermute(front, "ka", outer_back)
    beside_front = lax.ppermute(front, "ka", ring_back)
    rear = load(orbitals, 1)
    beyond_rear = lax.ppermute(rear, "ka", outer_back)
    beside_rear = lax.ppermute(rear, "ka", ring_back)
    own = (front, rear)
    gauge_half = lax.dynamic_index_in_dim(gauge.reshape(2, 2, 2, nb, nb), core, 2, keepdims=False)
    gauge_beyond = lax.ppermute(gauge_half, "ka", outer_back)
    gauge_beside = lax.ppermute(gauge_half, "ka", ring_back)

    fractions = grid_fractions(grid_part * plane_count, plane_count, plane_count * ga_count)
    my_table = lax.dynamic_slice_in_dim(neighbour, device * kloc, kloc, 0) % kloc
    my_shift = lax.dynamic_slice_in_dim(wrap_shift, device * kloc, kloc, 0)
    slots = jnp.arange(kloc, dtype=jnp.int32)
    local = jnp.stack([1 - core, 1 - core, core, core]).astype(jnp.int32)
    is_second = slots % 2

    def k_slots(direction, wanted):
        match = my_table[:, direction][:, None] == wanted[None, :]
        return jnp.sum(jnp.where(match, slots[:, None], 0), axis=0)

    order = local + 2 * is_second
    first_k = jnp.stack([k_slots(0, order), k_slots(1, local), k_slots(1, local + 2)])
    second_k = jnp.stack([k_slots(0, order), k_slots(2, local), k_slots(2, local + 2)])
    ks = jnp.where(is_second == 0, first_k, second_k).reshape(-1)
    locals_ = jnp.tile(local, 3)
    meta = jnp.stack([locals_, ks, locals_, jnp.concatenate([order, local, local + 2])])

    angles = jnp.concatenate([phase_angles(my_shift[:, b, :], b, counts, fractions) for b in range(3)])
    cosines, sines = jnp.cos(angles), jnp.sin(angles)

    def halves(meta, base, directions, sources, late=()):
        give = correlate(meta, base, directions, cosines, sines, own, sources)
        give, *late = lax.optimization_barrier((give, *late))
        got = lax.ppermute(give, "ga", sibling)
        return got, correlate(meta, base + 2, directions, cosines, sines, own, sources), late

    got, keep, _ = halves(meta, 0, (0, 0), own)
    got_front, keep_front, _ = halves(meta, 4, (1, 2), (beside_front, beyond_front))
    coded = encode(jnp.concatenate([keep + got, keep_front + got_front], axis=0))
    other = lax.ppermute(coded, "ga", across)
    coded, beside_rear, beyond_rear = lax.optimization_barrier((coded, beside_rear, beyond_rear))
    got, keep, gauges = halves(meta, 8, (1, 2), (beside_rear, beyond_rear), (gauge_beside, gauge_beyond))
    other, got = lax.optimization_barrier((other, got))
    coded_rear = encode(keep + got)
    other_rear = lax.ppermute(coded_rear, "ga", across)

    first, adj_x, adj_y = rotate(
        meta, (2, 3, 6, 7), decode(coded) + decode(other), gauge, gauges, (None, None, (0, 0), (1, 0)),
        [[(0, 0), (1, 0), (2, 0), (3, 0), (0, 1), (1, 1)], [(2, 1)], [(3, 1)]],
    )
    last, adj_x_rear, adj_y_rear = rotate(
        meta, (10, 11), decode(coded_rear) + decode(other_rear), gauge, gauges, ((0, 1), (1, 1)),
        [[(0, 0), (1, 0)], [(0, 1)], [(1, 1)]],
    )
    adj_y = lax.ppermute(encode(jnp.concatenate([adj_y, adj_y_rear], axis=0)), "ka", outer_ahead)
    adj_x = lax.ppermute(encode(jnp.concatenate([adj_x, adj_x_rear], axis=0)), "ka", ring_ahead)
    fwd = jnp.concatenate([first, last], axis=0)
    fwd_sib = lax.ppermute(fwd, "ga", sibling)
    targets = [
        [(0, 0, i), (0, 0, i + 1), (0, 1, i + 4), (0, 2, i + 5), (1, 0, i), (1, 0, i + 1), (0, 1, i + 8), (0, 2, i + 9)]
        for i in (2, 0)
    ]
    outs = place(targets, meta, (fwd, fwd_sib), None)
    adj_x, adj_y, *outs = lax.optimization_barrier((adj_x, adj_y, *outs))
    adj = lax.optimization_barrier(jnp.concatenate([adj_x, adj_y], axis=0))
    adj_sib = lax.ppermute(adj, "ga", sibling)
    targets = [[(1, 1, i + 4), (1, 1, i + 8), (1, 2, i + 5), (1, 2, i + 9)] for i in (2, 0)]
    return tuple(place(targets, meta, (decode(adj), decode(adj_sib)), outs))


def solution(mesh):
    in_specs = (P(None, "ka", None, "ga"), P(None, "ka", None, None), P(), P())
    out_specs = (P(None, None, "ka", None, None), P(None, None, "ka", None, None))
    return jax.shard_map(shards, mesh=mesh, in_specs=in_specs, out_specs=out_specs, check_vma=False)
```

```python
import math

import jax
import jax.numpy as jnp
from jax import lax
from jax.experimental import pallas as pl
from jax.experimental.pallas import tpu as pltpu
from jax.sharding import PartitionSpec as P

KRING = 4
GY = 32
GZ = 32
F32 = jnp.float32
BF16 = jnp.bfloat16
SHIFT = 13
VMEM = pltpu.VMEM
CONTRACT_LAST = (((1,), (1,)), ((), ()))
CONTRACT_FIRST = (((0,), (0,)), ((), ()))


def grid_fractions(plane_first, plane_count, plane_total):
    point_index = jnp.arange(plane_count * GY * GZ, dtype=jnp.int32)
    plane = point_index // (GY * GZ) + plane_first
    middle = point_index // GZ % GY
    inner = point_index % GZ
    return [
        plane.astype(F32) / F32(plane_total),
        middle.astype(F32) / F32(GY),
        inner.astype(F32) / F32(GZ),
    ]


def phase_angles(shift_rows, direction, mesh_counts, fractions):
    total = jnp.zeros((shift_rows.shape[0], fractions[0].shape[0]), F32)
    for lattice in range(3):
        step = 1.0 / mesh_counts[lattice] if lattice == direction else 0.0
        wave = shift_rows[:, lattice].astype(F32) + F32(step)
        total = total + wave[:, None] * fractions[lattice][None, :]
    return F32(2.0 * math.pi) * total


def vmem(*arrays):
    return tuple(pltpu.with_memory_space_constraint(array, VMEM) for array in arrays)


def specs(*spaces):
    return [pl.BlockSpec(memory_space=space) for space in spaces]


def small(mib):
    return {
        "cost_estimate": pl.CostEstimate(flops=1, bytes_accessed=1, transcendentals=0),
        "compiler_params": pltpu.CompilerParams(vmem_limit_bytes=mib * 2**20),
    }


def load(orbitals, part):
    nb, points = orbitals.shape[2:]

    def body(orbitals, out, sems):
        copies = [
            pltpu.make_async_copy(
                orbitals.at[c, 2 * part + slot], out.at[c, slot * nb : (slot + 1) * nb], sems.at[2 * c + slot]
            )
            for c in range(2)
            for slot in range(2)
        ]
        for copy in copies:
            copy.start()
        for copy in copies:
            copy.wait()

    return pl.pallas_call(
        body,
        name="load",
        out_shape=VMEM((2, 2 * nb, points), BF16),
        in_specs=specs(pl.ANY),
        out_specs=specs(VMEM)[0],
        scratch_shapes=[pltpu.SemaphoreType.DMA((4,))],
        **small(2),
    )(pltpu.with_memory_space_constraint(orbitals, pltpu.HBM))


def correlate(meta, base, directions, cosines, sines, own, sources):
    nb = own[0].shape[1] // 2
    points = own[0].shape[2]

    def body(meta, cosines, sines, front, rear, first, second, out, arrived, left, phased, sems):
        copies = []
        for p, source in enumerate((first, second)):
            rows = pl.ds(pl.multiple_of(meta[0, base + p] * nb, nb), nb)
            copies += [pltpu.make_async_copy(source.at[c, rows], arrived.at[p, c], sems.at[p, c]) for c in range(2)]
        for copy in copies:
            copy.start()
        for p in range(2):
            k = meta[1, base + p]
            lefts, shifted = left.at[p], phased.at[p]
            for half, ref in enumerate((front, rear)):

                @pl.when(k // 2 == half)
                def _():
                    start = pl.multiple_of((k - 2 * half) * nb, nb)
                    for c in range(2):
                        lefts[c * nb : (c + 1) * nb, :] = ref[c, pl.ds(start, nb), :]

            row = directions[p] * 4 + k
            cosine = cosines[pl.ds(row, 1), :]
            sine = sines[pl.ds(row, 1), :]
            for c in range(2):
                copies[2 * p + c].wait()
            source_re = arrived[p, 0].astype(F32)
            source_im = arrived[p, 1].astype(F32)
            shifted[0:nb, :] = (cosine * source_re + sine * source_im).astype(BF16)
            shifted[nb:, :] = (cosine * source_im - sine * source_re).astype(BF16)
            full = lax.dot_general(lefts[...], shifted[...], CONTRACT_LAST, preferred_element_type=F32)
            out[p, 0] = full[:nb, :nb] + full[nb:, nb:]
            out[p, 1] = full[:nb, nb:] - full[nb:, :nb]

    return pl.pallas_call(
        body,
        name="correlate",
        out_shape=VMEM((2, 2, nb, nb), F32),
        in_specs=specs(pltpu.SMEM, *[VMEM] * 4, pl.ANY, pl.ANY),
        out_specs=specs(VMEM)[0],
        scratch_shapes=[
            VMEM((2, 2, nb, points), BF16),
            VMEM((2, 2 * nb, points), BF16),
            VMEM((2, 2 * nb, points), BF16),
            pltpu.SemaphoreType.DMA((2, 2)),
        ],
        **small(8),
    )(meta, *vmem(cosines, sines, *own), *sources)


def split_parts(values):
    high = values.astype(BF16)
    low = (values - high.astype(F32)).astype(BF16)
    return high, low


def rotate_pair(raw_parts, left, right):
    nb = left[0].shape[0]
    raw_re, raw_im = [jnp.concatenate(split_parts(part), axis=1) for part in raw_parts]
    raw = jnp.concatenate([raw_re, raw_im], axis=0)
    wide = jnp.concatenate(right, axis=1)
    prod = jnp.dot(raw, jnp.concatenate([wide, wide], axis=0), preferred_element_type=F32)
    temp_re = prod[:nb, :nb] - prod[nb:, nb:]
    temp_im = prod[:nb, nb:] + prod[nb:, :nb]
    re_high, re_low = split_parts(temp_re)
    im_high, im_low = split_parts(temp_im)
    temp = jnp.concatenate(
        [jnp.concatenate([re_high, im_high], axis=1), jnp.concatenate([re_low, im_low], axis=1)], axis=0
    )
    tall = jnp.concatenate(left, axis=1)
    prod = lax.dot_general(
        jnp.concatenate([tall, tall], axis=0), temp, CONTRACT_FIRST, preferred_element_type=F32
    )
    return prod[:nb, :nb] + prod[nb:, nb:], prod[:nb, nb:] - prod[nb:, :nb]


def encode(chip):
    pairs, _, nb, _ = chip.shape
    largest = jnp.max(jnp.abs(chip), axis=(1, 2, 3))
    exponent = jnp.floor(jnp.log2(jnp.maximum(largest, F32(1e-30))))
    scaled = chip * jnp.exp2(F32(SHIFT) - exponent)[:, None, None, None]
    tail = jnp.broadcast_to(exponent[:, None, None], (pairs, 8, nb))
    coded = jnp.concatenate([scaled.reshape(pairs, 2 * nb, nb), tail], axis=1).astype(jnp.float16)
    return lax.optimization_barrier(coded)


def decode(coded):
    pairs, rows, nb = coded.shape
    exponent = coded[:, rows - 1, 0].astype(F32)
    values = coded[:, : 2 * nb].astype(F32) * jnp.exp2(exponent - F32(SHIFT))[:, None, None]
    return values.reshape(pairs, 2, nb, nb)


def rotate(meta, columns, raw, gauge, packed, right_of, layout):
    nb = gauge.shape[2]
    pairs = len(right_of)

    def body(slots, raw, gauge, *refs):
        payloads, outs = refs[: len(packed)], refs[len(packed) :]
        for p in range(pairs):
            k = slots[1, columns[p]]
            if right_of[p] is None:
                right = [gauge[c, slots[3, columns[p]]] for c in range(2)]
            else:
                right = [payloads[right_of[p][0]][c, right_of[p][1]] for c in range(2)]
            out_re, out_im = rotate_pair([raw[p, c] for c in range(2)], [gauge[c, k] for c in range(2)], right)
            for out, rows in zip(outs, layout):
                for row, (pair, adjoint) in enumerate(rows):
                    if pair == p and adjoint:
                        out[row, 0] = out_re.T
                        out[row, 1] = -out_im.T
                    elif pair == p:
                        out[row, 0] = out_re
                        out[row, 1] = out_im

    return pl.pallas_call(
        body,
        name="rotate",
        out_shape=tuple(VMEM((len(rows), 2, nb, nb), F32) for rows in layout),
        in_specs=specs(pltpu.SMEM, *[VMEM] * (2 + len(packed))),
        out_specs=tuple(specs(*[VMEM] * len(layout))),
        **small(8),
    )(meta, *vmem(raw, gauge, *packed))


def place(targets, meta, blocks, outs):
    nb = blocks[0].shape[-1]
    shape = jax.ShapeDtypeStruct((3, 2, 4, nb, nb), F32)
    previous = () if outs is None else tuple(outs)
    def body(slots, *refs):
        sems = refs[-1]
        into = refs[-3:-1]
        copies = []
        for block, rows in zip(refs, targets):
            for n, (output, direction, column) in enumerate(rows):
                target = into[output].at[direction, :, slots[3 if output else 1, column]]
                copies.append(pltpu.make_async_copy(block.at[n], target, sems.at[len(copies)]))
        for copy in copies:
            copy.start()
        for copy in copies:
            copy.wait()

    count = len(blocks)
    total = sum(len(rows) for rows in targets)
    return pl.pallas_call(
        body,
        out_shape=(shape, shape),
        name="place",
        in_specs=specs(pltpu.SMEM, *[VMEM] * count, *[pl.ANY] * len(previous)),
        out_specs=tuple(specs(pl.ANY, pl.ANY)),
        scratch_shapes=[pltpu.SemaphoreType.DMA((total,))],
        input_output_aliases={1 + count: 0, 2 + count: 1} if previous else {},
        **small(2),
    )(meta, *vmem(*blocks), *previous)


def shards(orbitals, gauge, neighbour, wrap_shift):
    kloc = orbitals.shape[1]
    grid_points = orbitals.shape[3]
    ka_count = lax.axis_size("ka")
    ga_count = lax.axis_size("ga")
    device = lax.axis_index("ka")
    grid_part = lax.axis_index("ga")
    core = grid_part % 2
    plane_count = grid_points // (GY * GZ)
    counts = (kloc, KRING, ka_count // KRING)

    ring_back = [(d, d // KRING * KRING + (d - 1) % KRING) for d in range(ka_count)]
    outer_back = [(d, (d - KRING) % ka_count) for d in range(ka_count)]
    ring_ahead = [(t, s) for s, t in ring_back]
    outer_ahead = [(t, s) for s, t in outer_back]
    sibling = [(g, g ^ 1) for g in range(ga_count)]
    across = [(g, g ^ 2) for g in range(ga_count)]

    nb = orbitals.shape[2]
    front = load(orbitals, 0)
    beyond_front = lax.ppermute(front, "ka", outer_back)
    beside_front = lax.ppermute(front, "ka", ring_back)
    rear = load(orbitals, 1)
    beyond_rear = lax.ppermute(rear, "ka", outer_back)
    beside_rear = lax.ppermute(rear, "ka", ring_back)
    own = (front, rear)
    gauge_half = lax.dynamic_index_in_dim(gauge.reshape(2, 2, 2, nb, nb), core, 2, keepdims=False)
    gauge_beyond = lax.ppermute(gauge_half, "ka", outer_back)
    gauge_beside = lax.ppermute(gauge_half, "ka", ring_back)

    fractions = grid_fractions(grid_part * plane_count, plane_count, plane_count * ga_count)
    my_table = lax.dynamic_slice_in_dim(neighbour, device * kloc, kloc, 0) % kloc
    my_shift = lax.dynamic_slice_in_dim(wrap_shift, device * kloc, kloc, 0)
    slots = jnp.arange(kloc, dtype=jnp.int32)
    local = jnp.stack([1 - core, 1 - core, core, core]).astype(jnp.int32)
    is_second = slots % 2

    def k_slots(direction, wanted):
        match = my_table[:, direction][:, None] == wanted[None, :]
        return jnp.sum(jnp.where(match, slots[:, None], 0), axis=0)

    order = local + 2 * is_second
    first_k = jnp.stack([k_slots(0, order), k_slots(1, local), k_slots(1, local + 2)])
    second_k = jnp.stack([k_slots(0, order), k_slots(2, local), k_slots(2, local + 2)])
    ks = jnp.where(is_second == 0, first_k, second_k).reshape(-1)
    locals_ = jnp.tile(local, 3)
    meta = jnp.stack([locals_, ks, locals_, jnp.concatenate([order, local, local + 2])])

    angles = jnp.concatenate([phase_angles(my_shift[:, b, :], b, counts, fractions) for b in range(3)])
    cosines, sines = jnp.cos(angles), jnp.sin(angles)

    def halves(meta, base, directions, sources, late=()):
        give = correlate(meta, base, directions, cosines, sines, own, sources)
        give, *late = lax.optimization_barrier((give, *late))
        got = lax.ppermute(give, "ga", sibling)
        return got, correlate(meta, base + 2, directions, cosines, sines, own, sources), late

    got, keep, _ = halves(meta, 0, (0, 0), own)
    got_front, keep_front, _ = halves(meta, 4, (1, 2), (beside_front, beyond_front))
    coded = encode(jnp.concatenate([keep + got, keep_front + got_front], axis=0))
    other = lax.ppermute(coded, "ga", across)
    coded, beside_rear, beyond_rear = lax.optimization_barrier((coded, beside_rear, beyond_rear))
    got, keep, gauges = halves(meta, 8, (1, 2), (beside_rear, beyond_rear), (gauge_beside, gauge_beyond))
    other, got = lax.optimization_barrier((other, got))
    coded_rear = encode(keep + got)
    other_rear = lax.ppermute(coded_rear, "ga", across)

    first, adj_x, adj_y = rotate(
        meta, (2, 3, 6, 7), decode(coded) + decode(other), gauge, gauges, (None, None, (0, 0), (1, 0)),
        [[(0, 0), (1, 0), (2, 0), (3, 0), (0, 1), (1, 1)], [(2, 1)], [(3, 1)]],
    )
    last, adj_x_rear, adj_y_rear = rotate(
        meta, (10, 11), decode(coded_rear) + decode(other_rear), gauge, gauges, ((0, 1), (1, 1)),
        [[(0, 0), (1, 0)], [(0, 1)], [(1, 1)]],
    )
    adj_y = lax.ppermute(encode(jnp.concatenate([adj_y, adj_y_rear], axis=0)), "ka", outer_ahead)
    adj_x = lax.ppermute(encode(jnp.concatenate([adj_x, adj_x_rear], axis=0)), "ka", ring_ahead)
    first_sib = lax.ppermute(first, "ga", sibling)
    last_sib = lax.ppermute(last, "ga", sibling)
    targets = [
        [(0, 0, i), (0, 0, i + 1), (0, 1, i + 4), (0, 2, i + 5), (1, 0, i), (1, 0, i + 1)] for i in (2, 0)
    ]
    outs = place(targets, meta, (first, first_sib), None)
    adj_x, adj_y, *outs = lax.optimization_barrier((adj_x, adj_y, *outs))
    adj = lax.optimization_barrier(jnp.concatenate([adj_x, adj_y], axis=0))
    adj_sib = lax.ppermute(adj, "ga", sibling)
    targets = [[(1, 1, i + 4), (1, 1, i + 8), (1, 2, i + 5), (1, 2, i + 9)] for i in (2, 0)]
    targets += [[(0, 1, i + 8), (0, 2, i + 9)] for i in (2, 0)]
    return tuple(place(targets, meta, (decode(adj), decode(adj_sib), last, last_sib), outs))


def solution(mesh):
    in_specs = (P(None, "ka", None, "ga"), P(None, "ka", None, None), P(), P())
    out_specs = (P(None, None, "ka", None, None), P(None, None, "ka", None, None))
    return jax.shard_map(shards, mesh=mesh, in_specs=in_specs, out_specs=out_specs, check_vma=False)
```

```python
import math

import jax
import jax.numpy as jnp
from jax import lax
from jax.experimental import pallas as pl
from jax.experimental.pallas import tpu as pltpu
from jax.sharding import PartitionSpec as P

KRING = 4
GY = 32
GZ = 32
F32 = jnp.float32
BF16 = jnp.bfloat16
SHIFT = 13
VMEM = pltpu.VMEM
CONTRACT_LAST = (((1,), (1,)), ((), ()))
CONTRACT_FIRST = (((0,), (0,)), ((), ()))


def grid_fractions(plane_first, plane_count, plane_total):
    point_index = jnp.arange(plane_count * GY * GZ, dtype=jnp.int32)
    plane = point_index // (GY * GZ) + plane_first
    middle = point_index // GZ % GY
    inner = point_index % GZ
    return [
        plane.astype(F32) / F32(plane_total),
        middle.astype(F32) / F32(GY),
        inner.astype(F32) / F32(GZ),
    ]


def phase_angles(shift_rows, direction, mesh_counts, fractions):
    total = jnp.zeros((shift_rows.shape[0], fractions[0].shape[0]), F32)
    for lattice in range(3):
        step = 1.0 / mesh_counts[lattice] if lattice == direction else 0.0
        wave = shift_rows[:, lattice].astype(F32) + F32(step)
        total = total + wave[:, None] * fractions[lattice][None, :]
    return F32(2.0 * math.pi) * total


def vmem(*arrays):
    return tuple(pltpu.with_memory_space_constraint(array, VMEM) for array in arrays)


def specs(*spaces):
    return [pl.BlockSpec(memory_space=space) for space in spaces]


def small(mib):
    return {
        "cost_estimate": pl.CostEstimate(flops=1, bytes_accessed=1, transcendentals=0),
        "compiler_params": pltpu.CompilerParams(vmem_limit_bytes=mib * 2**20),
    }


def load(orbitals, part):
    nb, points = orbitals.shape[2:]

    def body(orbitals, out, sems):
        copies = [
            pltpu.make_async_copy(
                orbitals.at[c, 2 * part + slot], out.at[c, slot * nb : (slot + 1) * nb], sems.at[2 * c + slot]
            )
            for c in range(2)
            for slot in range(2)
        ]
        for copy in copies:
            copy.start()
        for copy in copies:
            copy.wait()

    return pl.pallas_call(
        body,
        name="load",
        out_shape=VMEM((2, 2 * nb, points), BF16),
        in_specs=specs(pl.ANY),
        out_specs=specs(VMEM)[0],
        scratch_shapes=[pltpu.SemaphoreType.DMA((4,))],
        **small(2),
    )(pltpu.with_memory_space_constraint(orbitals, pltpu.HBM))


def correlate(meta, base, directions, cosines, sines, own, sources, arrived=None):
    nb = own[0].shape[1] // 2
    points = own[0].shape[2]

    copying = arrived is None

    def body(meta, cosines, sines, front, rear, *refs):
        copies = []
        if copying:
            first, second, out, ahead, left, phased, arrived, sems = refs
            for n, (column, into) in enumerate(((base, arrived), (base + 2, ahead))):
                for p, source in enumerate((first, second)):
                    rows = pl.ds(pl.multiple_of(meta[0, column + p] * nb, nb), nb)
                    for c in range(2):
                        copies.append(pltpu.make_async_copy(source.at[c, rows], into.at[p, c], sems.at[n, p, c]))
            for copy in copies:
                copy.start()
        else:
            arrived, out, left, phased = refs
        for p in range(2):
            k = meta[1, base + p]
            lefts, shifted = left.at[p], phased.at[p]
            for half, ref in enumerate((front, rear)):

                @pl.when(k // 2 == half)
                def _():
                    start = pl.multiple_of((k - 2 * half) * nb, nb)
                    for c in range(2):
                        lefts[c * nb : (c + 1) * nb, :] = ref[c, pl.ds(start, nb), :]

            row = directions[p] * 4 + k
            cosine = cosines[pl.ds(row, 1), :]
            sine = sines[pl.ds(row, 1), :]
            for copy in copies[2 * p : 2 * p + 2]:
                copy.wait()
            source_re = arrived[p, 0].astype(F32)
            source_im = arrived[p, 1].astype(F32)
            shifted[0:nb, :] = (cosine * source_re + sine * source_im).astype(BF16)
            shifted[nb:, :] = (cosine * source_im - sine * source_re).astype(BF16)
            full = lax.dot_general(lefts[...], shifted[...], CONTRACT_LAST, preferred_element_type=F32)
            out[p, 0] = full[:nb, :nb] + full[nb:, nb:]
            out[p, 1] = full[:nb, nb:] - full[nb:, :nb]
        for copy in copies[4:]:
            copy.wait()

    result = VMEM((2, 2, nb, nb), F32)
    blocks = VMEM((2, 2, nb, points), BF16)
    scratch = [VMEM((2, 2 * nb, points), BF16), VMEM((2, 2 * nb, points), BF16)]
    if copying:
        scratch += [blocks, pltpu.SemaphoreType.DMA((2, 2, 2))]
    return pl.pallas_call(
        body,
        name="correlate",
        out_shape=(result, blocks) if copying else result,
        in_specs=specs(pltpu.SMEM, *[VMEM] * 4, *([pl.ANY, pl.ANY] if copying else [VMEM])),
        out_specs=tuple(specs(VMEM, VMEM)) if copying else specs(VMEM)[0],
        scratch_shapes=scratch,
        **small(8),
    )(meta, *vmem(cosines, sines, *own), *(sources if copying else vmem(arrived)))


def split_parts(values):
    high = values.astype(BF16)
    low = (values - high.astype(F32)).astype(BF16)
    return high, low


def rotate_pair(raw_parts, left, right):
    nb = left[0].shape[0]
    raw_re, raw_im = [jnp.concatenate(split_parts(part), axis=1) for part in raw_parts]
    raw = jnp.concatenate([raw_re, raw_im], axis=0)
    wide = jnp.concatenate(right, axis=1)
    prod = jnp.dot(raw, jnp.concatenate([wide, wide], axis=0), preferred_element_type=F32)
    temp_re = prod[:nb, :nb] - prod[nb:, nb:]
    temp_im = prod[:nb, nb:] + prod[nb:, :nb]
    re_high, re_low = split_parts(temp_re)
    im_high, im_low = split_parts(temp_im)
    temp = jnp.concatenate(
        [jnp.concatenate([re_high, im_high], axis=1), jnp.concatenate([re_low, im_low], axis=1)], axis=0
    )
    tall = jnp.concatenate(left, axis=1)
    prod = lax.dot_general(
        jnp.concatenate([tall, tall], axis=0), temp, CONTRACT_FIRST, preferred_element_type=F32
    )
    return prod[:nb, :nb] + prod[nb:, nb:], prod[:nb, nb:] - prod[nb:, :nb]


def encode(chip):
    pairs, _, nb, _ = chip.shape
    largest = jnp.max(jnp.abs(chip), axis=(1, 2, 3))
    exponent = jnp.floor(jnp.log2(jnp.maximum(largest, F32(1e-30))))
    scaled = chip * jnp.exp2(F32(SHIFT) - exponent)[:, None, None, None]
    tail = jnp.broadcast_to(exponent[:, None, None], (pairs, 8, nb))
    coded = jnp.concatenate([scaled.reshape(pairs, 2 * nb, nb), tail], axis=1).astype(jnp.float16)
    return lax.optimization_barrier(coded)


def decode(coded):
    pairs, rows, nb = coded.shape
    exponent = coded[:, rows - 1, 0].astype(F32)
    values = coded[:, : 2 * nb].astype(F32) * jnp.exp2(exponent - F32(SHIFT))[:, None, None]
    return values.reshape(pairs, 2, nb, nb)


def rotate(meta, columns, raw, gauge, packed, right_of, layout):
    nb = gauge.shape[2]
    pairs = len(right_of)

    def body(slots, raw, gauge, *refs):
        payloads, outs = refs[: len(packed)], refs[len(packed) :]
        for p in range(pairs):
            k = slots[1, columns[p]]
            if right_of[p] is None:
                right = [gauge[c, slots[3, columns[p]]] for c in range(2)]
            else:
                right = [payloads[right_of[p][0]][c, right_of[p][1]] for c in range(2)]
            out_re, out_im = rotate_pair([raw[p, c] for c in range(2)], [gauge[c, k] for c in range(2)], right)
            for out, rows in zip(outs, layout):
                for row, (pair, adjoint) in enumerate(rows):
                    if pair == p and adjoint:
                        out[row, 0] = out_re.T
                        out[row, 1] = -out_im.T
                    elif pair == p:
                        out[row, 0] = out_re
                        out[row, 1] = out_im

    return pl.pallas_call(
        body,
        name="rotate",
        out_shape=tuple(VMEM((len(rows), 2, nb, nb), F32) for rows in layout),
        in_specs=specs(pltpu.SMEM, *[VMEM] * (2 + len(packed))),
        out_specs=tuple(specs(*[VMEM] * len(layout))),
        **small(8),
    )(meta, *vmem(raw, gauge, *packed))


def place(targets, meta, blocks, outs):
    nb = blocks[0].shape[-1]
    shape = jax.ShapeDtypeStruct((3, 2, 4, nb, nb), F32)
    previous = () if outs is None else tuple(outs)
    def body(slots, *refs):
        sems = refs[-1]
        into = refs[-3:-1]
        copies = []
        for block, rows in zip(refs, targets):
            for n, (output, direction, column) in enumerate(rows):
                target = into[output].at[direction, :, slots[3 if output else 1, column]]
                copies.append(pltpu.make_async_copy(block.at[n], target, sems.at[len(copies)]))
        for copy in copies:
            copy.start()
        for copy in copies:
            copy.wait()

    count = len(blocks)
    total = sum(len(rows) for rows in targets)
    return pl.pallas_call(
        body,
        out_shape=(shape, shape),
        name="place",
        in_specs=specs(pltpu.SMEM, *[VMEM] * count, *[pl.ANY] * len(previous)),
        out_specs=tuple(specs(pl.ANY, pl.ANY)),
        scratch_shapes=[pltpu.SemaphoreType.DMA((total,))],
        input_output_aliases={1 + count: 0, 2 + count: 1} if previous else {},
        **small(2),
    )(meta, *vmem(*blocks), *previous)


def shards(orbitals, gauge, neighbour, wrap_shift):
    kloc = orbitals.shape[1]
    grid_points = orbitals.shape[3]
    ka_count = lax.axis_size("ka")
    ga_count = lax.axis_size("ga")
    device = lax.axis_index("ka")
    grid_part = lax.axis_index("ga")
    core = grid_part % 2
    plane_count = grid_points // (GY * GZ)
    counts = (kloc, KRING, ka_count // KRING)

    ring_back = [(d, d // KRING * KRING + (d - 1) % KRING) for d in range(ka_count)]
    outer_back = [(d, (d - KRING) % ka_count) for d in range(ka_count)]
    ring_ahead = [(t, s) for s, t in ring_back]
    outer_ahead = [(t, s) for s, t in outer_back]
    sibling = [(g, g ^ 1) for g in range(ga_count)]
    across = [(g, g ^ 2) for g in range(ga_count)]

    nb = orbitals.shape[2]
    front = load(orbitals, 0)
    beyond_front = lax.ppermute(front, "ka", outer_back)
    beside_front = lax.ppermute(front, "ka", ring_back)
    rear = load(orbitals, 1)
    beyond_rear = lax.ppermute(rear, "ka", outer_back)
    beside_rear = lax.ppermute(rear, "ka", ring_back)
    own = (front, rear)
    gauge_half = lax.dynamic_index_in_dim(gauge.reshape(2, 2, 2, nb, nb), core, 2, keepdims=False)
    gauge_beyond = lax.ppermute(gauge_half, "ka", outer_back)
    gauge_beside = lax.ppermute(gauge_half, "ka", ring_back)

    fractions = grid_fractions(grid_part * plane_count, plane_count, plane_count * ga_count)
    my_table = lax.dynamic_slice_in_dim(neighbour, device * kloc, kloc, 0) % kloc
    my_shift = lax.dynamic_slice_in_dim(wrap_shift, device * kloc, kloc, 0)
    slots = jnp.arange(kloc, dtype=jnp.int32)
    local = jnp.stack([1 - core, 1 - core, core, core]).astype(jnp.int32)
    is_second = slots % 2

    def k_slots(direction, wanted):
        match = my_table[:, direction][:, None] == wanted[None, :]
        return jnp.sum(jnp.where(match, slots[:, None], 0), axis=0)

    order = local + 2 * is_second
    first_k = jnp.stack([k_slots(0, order), k_slots(1, local), k_slots(1, local + 2)])
    second_k = jnp.stack([k_slots(0, order), k_slots(2, local), k_slots(2, local + 2)])
    ks = jnp.where(is_second == 0, first_k, second_k).reshape(-1)
    locals_ = jnp.tile(local, 3)
    meta = jnp.stack([locals_, ks, locals_, jnp.concatenate([order, local, local + 2])])

    angles = jnp.concatenate([phase_angles(my_shift[:, b, :], b, counts, fractions) for b in range(3)])
    cosines, sines = jnp.cos(angles), jnp.sin(angles)

    def halves(meta, base, directions, sources, late=()):
        give, ahead = correlate(meta, base, directions, cosines, sines, own, sources)
        give, *late = lax.optimization_barrier((give, *late))
        got = lax.ppermute(give, "ga", sibling)
        return got, correlate(meta, base + 2, directions, cosines, sines, own, None, ahead), late

    got, keep, _ = halves(meta, 0, (0, 0), own)
    got_front, keep_front, _ = halves(meta, 4, (1, 2), (beside_front, beyond_front))
    coded = encode(jnp.concatenate([keep + got, keep_front + got_front], axis=0))
    other = lax.ppermute(coded, "ga", across)
    coded, beside_rear, beyond_rear = lax.optimization_barrier((coded, beside_rear, beyond_rear))
    got, keep, gauges = halves(meta, 8, (1, 2), (beside_rear, beyond_rear), (gauge_beside, gauge_beyond))
    other, got = lax.optimization_barrier((other, got))
    coded_rear = encode(keep + got)
    other_rear = lax.ppermute(coded_rear, "ga", across)

    first, adj_x, adj_y = rotate(
        meta, (2, 3, 6, 7), decode(coded) + decode(other), gauge, gauges, (None, None, (0, 0), (1, 0)),
        [[(0, 0), (1, 0), (2, 0), (3, 0), (0, 1), (1, 1)], [(2, 1)], [(3, 1)]],
    )
    last, adj_x_rear, adj_y_rear = rotate(
        meta, (10, 11), decode(coded_rear) + decode(other_rear), gauge, gauges, ((0, 1), (1, 1)),
        [[(0, 0), (1, 0)], [(0, 1)], [(1, 1)]],
    )
    adj_y = lax.ppermute(encode(jnp.concatenate([adj_y, adj_y_rear], axis=0)), "ka", outer_ahead)
    adj_x = lax.ppermute(encode(jnp.concatenate([adj_x, adj_x_rear], axis=0)), "ka", ring_ahead)
    first_sib = lax.ppermute(first, "ga", sibling)
    last_sib = lax.ppermute(last, "ga", sibling)
    targets = [
        [(0, 0, i), (0, 0, i + 1), (0, 1, i + 4), (0, 2, i + 5), (1, 0, i), (1, 0, i + 1)] for i in (2, 0)
    ]
    outs = place(targets, meta, (first, first_sib), None)
    adj_x, adj_y, *outs = lax.optimization_barrier((adj_x, adj_y, *outs))
    adj = lax.optimization_barrier(jnp.concatenate([adj_x, adj_y], axis=0))
    adj_sib = lax.ppermute(adj, "ga", sibling)
    targets = [[(1, 1, i + 4), (1, 1, i + 8), (1, 2, i + 5), (1, 2, i + 9)] for i in (2, 0)]
    targets += [[(0, 1, i + 8), (0, 2, i + 9)] for i in (2, 0)]
    return tuple(place(targets, meta, (decode(adj), decode(adj_sib), last, last_sib), outs))


def solution(mesh):
    in_specs = (P(None, "ka", None, "ga"), P(None, "ka", None, None), P(), P())
    out_specs = (P(None, None, "ka", None, None), P(None, None, "ka", None, None))
    return jax.shard_map(shards, mesh=mesh, in_specs=in_specs, out_specs=out_specs, check_vma=False)
```

```python
import math

import jax
import jax.numpy as jnp
from jax import lax
from jax.experimental import pallas as pl
from jax.experimental.pallas import tpu as pltpu
from jax.sharding import PartitionSpec as P

KRING = 4
GY = 32
GZ = 32
F32 = jnp.float32
BF16 = jnp.bfloat16
SHIFT = 13
VMEM = pltpu.VMEM
CONTRACT_LAST = (((1,), (1,)), ((), ()))
CONTRACT_FIRST = (((0,), (0,)), ((), ()))


def grid_fractions(plane_first, plane_count, plane_total):
    point_index = jnp.arange(plane_count * GY * GZ, dtype=jnp.int32)
    plane = point_index // (GY * GZ) + plane_first
    middle = point_index // GZ % GY
    inner = point_index % GZ
    return [
        plane.astype(F32) / F32(plane_total),
        middle.astype(F32) / F32(GY),
        inner.astype(F32) / F32(GZ),
    ]


def phase_angles(shift_rows, direction, mesh_counts, fractions):
    total = jnp.zeros((shift_rows.shape[0], fractions[0].shape[0]), F32)
    for lattice in range(3):
        step = 1.0 / mesh_counts[lattice] if lattice == direction else 0.0
        wave = shift_rows[:, lattice].astype(F32) + F32(step)
        total = total + wave[:, None] * fractions[lattice][None, :]
    return F32(2.0 * math.pi) * total


def vmem(*arrays):
    return tuple(pltpu.with_memory_space_constraint(array, VMEM) for array in arrays)


def specs(*spaces):
    return [pl.BlockSpec(memory_space=space) for space in spaces]


def small(mib):
    return {
        "cost_estimate": pl.CostEstimate(flops=1, bytes_accessed=1, transcendentals=0),
        "compiler_params": pltpu.CompilerParams(vmem_limit_bytes=mib * 2**20),
    }


def load(orbitals, part):
    nb, points = orbitals.shape[2:]

    def body(orbitals, out, sems):
        copies = [
            pltpu.make_async_copy(
                orbitals.at[c, 2 * part + slot], out.at[c, slot * nb : (slot + 1) * nb], sems.at[2 * c + slot]
            )
            for c in range(2)
            for slot in range(2)
        ]
        for copy in copies:
            copy.start()
        for copy in copies:
            copy.wait()

    return pl.pallas_call(
        body,
        name="load",
        out_shape=VMEM((2, 2 * nb, points), BF16),
        in_specs=specs(pl.ANY),
        out_specs=specs(VMEM)[0],
        scratch_shapes=[pltpu.SemaphoreType.DMA((4,))],
        **small(2),
    )(pltpu.with_memory_space_constraint(orbitals, pltpu.HBM))


def correlate(meta, base, directions, cosines, sines, own, sources, arrived=None):
    nb = own[0].shape[1] // 2
    points = own[0].shape[2]

    copying = arrived is None

    def body(meta, cosines, sines, front, rear, *refs):
        copies = []
        if copying:
            first, second, out, ahead, left, phased, arrived, sems = refs
            for n, (column, into) in enumerate(((base, arrived), (base + 2, ahead))):
                for p, source in enumerate((first, second)):
                    rows = pl.ds(pl.multiple_of(meta[0, column + p] * nb, nb), nb)
                    for c in range(2):
                        copies.append(pltpu.make_async_copy(source.at[c, rows], into.at[p, c], sems.at[n, p, c]))
            for copy in copies:
                copy.start()
        else:
            arrived, out, left, phased = refs
        for p in range(2):
            k = meta[1, base + p]
            lefts, shifted = left.at[p], phased.at[p]
            for half, ref in enumerate((front, rear)):

                @pl.when(k // 2 == half)
                def _():
                    start = pl.multiple_of((k - 2 * half) * nb, nb)
                    for c in range(2):
                        lefts[c * nb : (c + 1) * nb, :] = ref[c, pl.ds(start, nb), :]

            row = directions[p] * 4 + k
            cosine = cosines[pl.ds(row, 1), :]
            sine = sines[pl.ds(row, 1), :]
            for copy in copies[2 * p : 2 * p + 2]:
                copy.wait()
            source_re = arrived[p, 0].astype(F32)
            source_im = arrived[p, 1].astype(F32)
            shifted[0:nb, :] = (cosine * source_re + sine * source_im).astype(BF16)
            shifted[nb:, :] = (cosine * source_im - sine * source_re).astype(BF16)
            full = lax.dot_general(lefts[...], shifted[...], CONTRACT_LAST, preferred_element_type=F32)
            out[p, 0] = full[:nb, :nb] + full[nb:, nb:]
            out[p, 1] = full[:nb, nb:] - full[nb:, :nb]
        for copy in copies[4:]:
            copy.wait()

    result = VMEM((2, 2, nb, nb), F32)
    blocks = VMEM((2, 2, nb, points), BF16)
    scratch = [VMEM((2, 2 * nb, points), BF16), VMEM((2, 2 * nb, points), BF16)]
    if copying:
        scratch += [blocks, pltpu.SemaphoreType.DMA((2, 2, 2))]
    return pl.pallas_call(
        body,
        name="correlate",
        out_shape=(result, blocks) if copying else result,
        in_specs=specs(pltpu.SMEM, *[VMEM] * 4, *([pl.ANY, pl.ANY] if copying else [VMEM])),
        out_specs=tuple(specs(VMEM, VMEM)) if copying else specs(VMEM)[0],
        scratch_shapes=scratch,
        **small(8),
    )(meta, *vmem(cosines, sines, *own), *(sources if copying else vmem(arrived)))


def split_parts(values):
    high = values.astype(BF16)
    low = (values - high.astype(F32)).astype(BF16)
    return high, low


def rotate_pair(raw_parts, left, right):
    nb = left[0].shape[0]
    raw_re, raw_im = [jnp.concatenate(split_parts(part), axis=1) for part in raw_parts]
    raw = jnp.concatenate([raw_re, raw_im], axis=0)
    wide = jnp.concatenate(right, axis=1)
    prod = jnp.dot(raw, jnp.concatenate([wide, wide], axis=0), preferred_element_type=F32)
    temp_re = prod[:nb, :nb] - prod[nb:, nb:]
    temp_im = prod[:nb, nb:] + prod[nb:, :nb]
    re_high, re_low = split_parts(temp_re)
    im_high, im_low = split_parts(temp_im)
    temp = jnp.concatenate(
        [jnp.concatenate([re_high, im_high], axis=1), jnp.concatenate([re_low, im_low], axis=1)], axis=0
    )
    tall = jnp.concatenate(left, axis=1)
    prod = lax.dot_general(
        jnp.concatenate([tall, tall], axis=0), temp, CONTRACT_FIRST, preferred_element_type=F32
    )
    return prod[:nb, :nb] + prod[nb:, nb:], prod[:nb, nb:] - prod[nb:, :nb]


def encode(chip):
    pairs, _, nb, _ = chip.shape
    largest = jnp.max(jnp.abs(chip), axis=(1, 2, 3))
    exponent = jnp.floor(jnp.log2(jnp.maximum(largest, F32(1e-30))))
    scaled = chip * jnp.exp2(F32(SHIFT) - exponent)[:, None, None, None]
    tail = jnp.broadcast_to(exponent[:, None, None], (pairs, 8, nb))
    coded = jnp.concatenate([scaled.reshape(pairs, 2 * nb, nb), tail], axis=1).astype(jnp.float16)
    return lax.optimization_barrier(coded)


def decode(coded):
    pairs, rows, nb = coded.shape
    exponent = coded[:, rows - 1, 0].astype(F32)
    values = coded[:, : 2 * nb].astype(F32) * jnp.exp2(exponent - F32(SHIFT))[:, None, None]
    return values.reshape(pairs, 2, nb, nb)


def rotate(meta, columns, raw, gauge, packed, right_of, layout):
    nb = gauge.shape[2]
    pairs = len(right_of)

    def body(slots, raw, gauge, *refs):
        payloads, outs = refs[: len(packed)], refs[len(packed) :]
        for p in range(pairs):
            k = slots[1, columns[p]]
            if right_of[p] is None:
                right = [gauge[c, slots[3, columns[p]]] for c in range(2)]
            else:
                right = [payloads[right_of[p][0]][c, right_of[p][1]] for c in range(2)]
            out_re, out_im = rotate_pair([raw[p, c] for c in range(2)], [gauge[c, k] for c in range(2)], right)
            for out, rows in zip(outs, layout):
                for row, (pair, adjoint) in enumerate(rows):
                    if pair == p and adjoint:
                        out[row, 0] = out_re.T
                        out[row, 1] = -out_im.T
                    elif pair == p:
                        out[row, 0] = out_re
                        out[row, 1] = out_im

    return pl.pallas_call(
        body,
        name="rotate",
        out_shape=tuple(VMEM((len(rows), 2, nb, nb), F32) for rows in layout),
        in_specs=specs(pltpu.SMEM, *[VMEM] * (2 + len(packed))),
        out_specs=tuple(specs(*[VMEM] * len(layout))),
        **small(8),
    )(meta, *vmem(raw, gauge, *packed))


def place(targets, meta, blocks, outs):
    nb = blocks[0].shape[-1]
    shape = jax.ShapeDtypeStruct((3, 2, 4, nb, nb), F32)
    previous = () if outs is None else tuple(outs)
    def body(slots, *refs):
        sems = refs[-1]
        into = refs[-3:-1]
        copies = []
        for block, rows in zip(refs, targets):
            for n, (output, direction, column) in enumerate(rows):
                target = into[output].at[direction, :, slots[3 if output else 1, column]]
                copies.append(pltpu.make_async_copy(block.at[n], target, sems.at[len(copies)]))
        for copy in copies:
            copy.start()
        for copy in copies:
            copy.wait()

    count = len(blocks)
    total = sum(len(rows) for rows in targets)
    return pl.pallas_call(
        body,
        out_shape=(shape, shape),
        name="place",
        in_specs=specs(pltpu.SMEM, *[VMEM] * count, *[pl.ANY] * len(previous)),
        out_specs=tuple(specs(pl.ANY, pl.ANY)),
        scratch_shapes=[pltpu.SemaphoreType.DMA((total,))],
        input_output_aliases={1 + count: 0, 2 + count: 1} if previous else {},
        **small(2),
    )(meta, *vmem(*blocks), *previous)


def shards(orbitals, gauge, neighbour, wrap_shift):
    kloc = orbitals.shape[1]
    grid_points = orbitals.shape[3]
    ka_count = lax.axis_size("ka")
    ga_count = lax.axis_size("ga")
    device = lax.axis_index("ka")
    grid_part = lax.axis_index("ga")
    core = grid_part % 2
    plane_count = grid_points // (GY * GZ)
    counts = (kloc, KRING, ka_count // KRING)

    ring_back = [(d, d // KRING * KRING + (d - 1) % KRING) for d in range(ka_count)]
    outer_back = [(d, (d - KRING) % ka_count) for d in range(ka_count)]
    ring_ahead = [(t, s) for s, t in ring_back]
    outer_ahead = [(t, s) for s, t in outer_back]
    sibling = [(g, g ^ 1) for g in range(ga_count)]
    across = [(g, g ^ 2) for g in range(ga_count)]

    nb = orbitals.shape[2]
    front = load(orbitals, 0)
    beyond_front = lax.ppermute(front, "ka", outer_back)
    beside_front = lax.ppermute(front, "ka", ring_back)
    rear = load(orbitals, 1)
    beyond_rear = lax.ppermute(rear, "ka", outer_back)
    beside_rear = lax.ppermute(rear, "ka", ring_back)
    own = (front, rear)
    gauge_half = lax.dynamic_index_in_dim(gauge.reshape(2, 2, 2, nb, nb), core, 2, keepdims=False)
    gauge_beyond = lax.ppermute(gauge_half, "ka", outer_back)
    gauge_beside = lax.ppermute(gauge_half, "ka", ring_back)

    fractions = grid_fractions(grid_part * plane_count, plane_count, plane_count * ga_count)
    my_table = lax.dynamic_slice_in_dim(neighbour, device * kloc, kloc, 0) % kloc
    my_shift = lax.dynamic_slice_in_dim(wrap_shift, device * kloc, kloc, 0)
    slots = jnp.arange(kloc, dtype=jnp.int32)
    local = jnp.stack([1 - core, 1 - core, core, core]).astype(jnp.int32)
    is_second = slots % 2

    def k_slots(direction, wanted):
        match = my_table[:, direction][:, None] == wanted[None, :]
        return jnp.sum(jnp.where(match, slots[:, None], 0), axis=0)

    order = local + 2 * is_second
    first_k = jnp.stack([k_slots(0, order), k_slots(1, local), k_slots(1, local + 2)])
    second_k = jnp.stack([k_slots(0, order), k_slots(2, local), k_slots(2, local + 2)])
    ks = jnp.where(is_second == 0, first_k, second_k).reshape(-1)
    locals_ = jnp.tile(local, 3)
    meta = jnp.stack([locals_, ks, locals_, jnp.concatenate([order, local, local + 2])])

    angles = jnp.concatenate([phase_angles(my_shift[:, b, :], b, counts, fractions) for b in range(3)])
    cosines, sines = jnp.cos(angles), jnp.sin(angles)

    def halves(meta, base, directions, sources, late=()):
        give, ahead = correlate(meta, base, directions, cosines, sines, own, sources)
        give, *late = lax.optimization_barrier((give, *late))
        got = lax.ppermute(give, "ga", sibling)
        return got, correlate(meta, base + 2, directions, cosines, sines, own, None, ahead), late

    got, keep, _ = halves(meta, 0, (0, 0), own)
    got_front, keep_front, _ = halves(meta, 4, (1, 2), (beside_front, beyond_front))
    coded = encode(jnp.concatenate([keep + got, keep_front + got_front], axis=0))
    other = lax.ppermute(coded, "ga", across)
    coded, beside_rear, beyond_rear = lax.optimization_barrier((coded, beside_rear, beyond_rear))
    got, keep, gauges = halves(meta, 8, (1, 2), (beside_rear, beyond_rear), (gauge_beside, gauge_beyond))
    other, got = lax.optimization_barrier((other, got))
    coded_rear = encode(keep + got)
    other_rear = lax.ppermute(coded_rear, "ga", across)

    first, adj_x, adj_y = rotate(
        meta, (2, 3, 6, 7), decode(coded) + decode(other), gauge, gauges, (None, None, (0, 0), (1, 0)),
        [[(0, 0), (1, 0), (2, 0), (3, 0), (0, 1), (1, 1)], [(2, 1)], [(3, 1)]],
    )
    last, adj_x_rear, adj_y_rear = rotate(
        meta, (10, 11), decode(coded_rear) + decode(other_rear), gauge, gauges, ((0, 1), (1, 1)),
        [[(0, 0), (1, 0)], [(0, 1)], [(1, 1)]],
    )
    adjoints = encode(jnp.concatenate([adj_y, adj_y_rear, adj_x, adj_x_rear], axis=0))
    adj_y = lax.ppermute(adjoints[:2], "ka", outer_ahead)
    adj_x = lax.ppermute(adjoints[2:], "ka", ring_ahead)
    first_sib = lax.ppermute(first, "ga", sibling)
    last_sib = lax.ppermute(last, "ga", sibling)
    targets = [
        [(0, 0, i), (0, 0, i + 1), (0, 1, i + 4), (0, 2, i + 5), (1, 0, i), (1, 0, i + 1)] for i in (2, 0)
    ]
    outs = place(targets, meta, (first, first_sib), None)
    adj_x, adj_y, *outs = lax.optimization_barrier((adj_x, adj_y, *outs))
    adj = lax.optimization_barrier(jnp.concatenate([adj_x, adj_y], axis=0))
    adj_sib = lax.ppermute(adj, "ga", sibling)
    targets = [[(1, 1, i + 4), (1, 1, i + 8), (1, 2, i + 5), (1, 2, i + 9)] for i in (2, 0)]
    targets += [[(0, 1, i + 8), (0, 2, i + 9)] for i in (2, 0)]
    return tuple(place(targets, meta, (decode(adj), decode(adj_sib), last, last_sib), outs))


def solution(mesh):
    in_specs = (P(None, "ka", None, "ga"), P(None, "ka", None, None), P(), P())
    out_specs = (P(None, None, "ka", None, None), P(None, None, "ka", None, None))
    return jax.shard_map(shards, mesh=mesh, in_specs=in_specs, out_specs=out_specs, check_vma=False)
```
